128 devices in a mesh: ctx: 32 (over x, z, core), tp: 4 (over y).
Axes of the slice: x: 4, y: 4, z: 4, core: 2. Of those that a mesh axis runs over, the one named last changes fastest.
Arguments:
- normed_input: bfloat16 [16384, 4096], P('ctx'), may hold values from -12 to 12
- w_query: bfloat16 [4096, 2048], P(None, 'tp'), may hold values from -0.09375 to 0.09375
- key_weight: bfloat16 [4096, 512], P(None, 'tp'), may hold values from -0.09375 to 0.09375
- value_weight: bfloat16 [4096, 512], P(None, 'tp'), may hold values from -0.09375 to 0.09375
- output_weight: bfloat16 [4096, 2048], P(None, 'tp'), may hold values from -0.125 to 0.125
- output_cotangent: bfloat16 [16384, 4096], P('ctx'), may hold values from -6 to 6
- piece_doc: int32 [2048], replicated, may hold values from 0 to 127, as said below
- piece_offset: int32 [2048], replicated, may hold values from 0 to 480, as said below
- doc_owner: int32 [128], replicated, may hold values from 0 to 31, as said below
Outputs:
- grad_in: bfloat16 [16384, 4096], P('ctx', 'tp')
- grad_query: bfloat16 [4096, 2048], P('ctx', 'tp')
- grad_key: bfloat16 [4096, 512], P('ctx', 'tp')
- grad_value: bfloat16 [4096, 512], P('ctx', 'tp')
- grad_out: bfloat16 [4096, 2048], P('ctx', 'tp')
The draws below stay inside these ranges and needn't reach their ends.
Inputs may be any that keep to these rules, and one draw needn't show every extreme that they name: `piece_doc`: every document has at least one piece; the pieces of one document, in increasing token order, have offsets 0, 8, 16 and so on. `piece_offset`: A piece belongs to the owner of its document. The pieces of the tokens of one index of ctx go to exactly 32 / 2 owners, exactly 32 tokens to each of them; so every owner receives 512 tokens. `doc_owner`: every device of ctx owns exactly 4 documents.
All inputs are finite; a program needn't handle non-finite values.
Results may differ from the reference program's by a relative error of at most 0.015.
Values may be sent and summed in bfloat16 or wider, within the bound.
No kernel may reach another device: no remote copies, remote signals or barrier semaphores. Data moves between devices by JAX's collectives and lax.ppermute only.
A program may use at most 128 MiB of HBM per device.

```python
import math
import jax
import jax.numpy as jnp
from jax import lax

MODEL_WIDTH = 4096
QUERY_HEAD_COUNT = 16
KV_HEAD_COUNT = 4
HEAD_SIZE = 128
PIECE = 8
DOCS_OWN = 4
TOKENS_PER_SHARD = 512
TOKENS = 16384
SLOTS = 32
NDOC = 128
N_CTX = 32


def layout_plan(key):
    base_key = jax.random.fold_in(key, 7101)
    half_count = N_CTX // 2
    per_device = TOKENS_PER_SHARD // PIECE
    per_slot = SLOTS // PIECE
    owner_cycle = jax.random.permutation(jax.random.fold_in(base_key, 1), N_CTX).astype(jnp.int32)
    sources = jnp.arange(N_CTX, dtype=jnp.int32)
    chosen = owner_cycle[(sources[:, None] + jnp.arange(half_count, dtype=jnp.int32)[None, :]) % N_CTX]
    listed = jnp.repeat(chosen, per_slot, axis=1)
    shuffle_keys = jax.random.split(jax.random.fold_in(base_key, 2), N_CTX)
    shuffled = jax.vmap(lambda subkey, listing: jax.random.permutation(subkey, listing))(shuffle_keys, listed)
    owner_flat = shuffled.reshape(-1).astype(jnp.int32)
    onehot = (owner_flat[:, None] == jnp.arange(N_CTX, dtype=jnp.int32)[None, :]).astype(jnp.int32)
    arrival = jnp.sum((jnp.cumsum(onehot, axis=0) - 1) * onehot, axis=1)
    cut_keys = jax.random.split(jax.random.fold_in(base_key, 3), N_CTX)

    def cuts_for(subkey):
        return jax.random.permutation(subkey, per_device - 1)[:DOCS_OWN - 1].astype(jnp.int32) + 1
    cut_points = jax.vmap(cuts_for)(cut_keys)
    cut_points = cut_points.at[0].set(jnp.arange(1, DOCS_OWN, dtype=jnp.int32))
    owner_cuts = cut_points[owner_flat]
    passed = owner_cuts <= arrival[:, None]
    doc_local = jnp.sum(passed.astype(jnp.int32), axis=1)
    doc_start = jnp.max(jnp.where(passed, owner_cuts, 0), axis=1)
    offsets = ((arrival - doc_start) * PIECE).astype(jnp.int32)
    labels = jax.random.permutation(jax.random.fold_in(base_key, 4), NDOC).astype(jnp.int32)
    piece_docs = labels[owner_flat * DOCS_OWN + doc_local]
    owners_of = jnp.arange(NDOC, dtype=jnp.int32) // DOCS_OWN
    owner_table = jnp.zeros((NDOC,), jnp.int32).at[labels].set(owners_of)
    return (piece_docs, offsets, owner_table)


def draw_piece_doc(key, part):
    return layout_plan(key)[0]


def draw_piece_offset(key, part):
    return layout_plan(key)[1]


def draw_doc_owner(key, part):
    return layout_plan(key)[2]


def draw_normed_input(key, part):
    normal_base = jnp.clip(jax.random.normal(jax.random.fold_in(key, 11), (TOKENS, MODEL_WIDTH), jnp.float32), -6.0, 6.0)
    return normal_base.astype(jnp.bfloat16)


def shard_levels(rng, extent, shards, low, largest):
    level, own = 1.0, jax.random.fold_in(rng, 6)
    for dim, shards_of in shards:
        steps = jnp.exp(jax.random.uniform(jax.random.fold_in(own, dim), (shards_of,), jnp.float32, low / len(shards), largest / len(shards)))
        level = level * jnp.repeat(steps, extent[dim] // shards_of).reshape([-1 if axis == dim else 1 for axis in range(len(extent))])
    return level


def normal_values(stream_key, dims, scale, limit, shards=(), held_as=jnp.bfloat16):
    array = jax.random.normal(stream_key, dims, jnp.float32) * scale
    if len(shards) > 0:
        array = shard_levels(stream_key, dims, shards, -0.22, 0.18) * array
    return jnp.clip(array, min=-limit, max=limit).astype(held_as)


def setup_inputs(seed: int = 0) -> dict:
    splits = jax.random.split(jax.random.key(seed), 10)
    normed_input = draw_normed_input(jax.random.fold_in(splits[9], 71), 0)
    w_query = normal_values(splits[1], (MODEL_WIDTH, QUERY_HEAD_COUNT * HEAD_SIZE), MODEL_WIDTH ** -0.5, 0.09375, ((1, 4),))
    key_weight = normal_values(splits[2], (MODEL_WIDTH, KV_HEAD_COUNT * HEAD_SIZE), MODEL_WIDTH ** -0.5, 0.09375, ((1, 4),))
    value_weight = normal_values(splits[3], (MODEL_WIDTH, KV_HEAD_COUNT * HEAD_SIZE), MODEL_WIDTH ** -0.5, 0.09375, ((1, 4),))
    output_weight = normal_values(splits[4], (MODEL_WIDTH, QUERY_HEAD_COUNT * HEAD_SIZE), (QUERY_HEAD_COUNT * HEAD_SIZE) ** -0.5, 0.125, ((1, 4),))
    output_cotangent = normal_values(splits[5], (TOKENS, MODEL_WIDTH), 1.0, 6.0, ((0, 32),))
    piece_doc = draw_piece_doc(jax.random.fold_in(splits[9], 71), 0)
    piece_offset = draw_piece_offset(jax.random.fold_in(splits[9], 71), 0)
    doc_owner = draw_doc_owner(jax.random.fold_in(splits[9], 71), 0)
    return {"normed_input": normed_input, "w_query": w_query, "key_weight": key_weight, "value_weight": value_weight, "output_weight": output_weight, "output_cotangent": output_cotangent, "piece_doc": piece_doc, "piece_offset": piece_offset, "doc_owner": doc_owner}


rope_base = 500000.0
fill_value = -1e+30

def apply_rotary(heads, positions, direction):
    half_width = heads.shape[-1] // 2
    frequency = rope_base ** (-2.0 * jnp.arange(half_width, dtype=jnp.float32) / heads.shape[-1])
    angles = positions.astype(jnp.float32)[:, None] * frequency[None, :]
    cosine = jnp.cos(angles)[:, None, :]
    sine_term = direction * jnp.sin(angles)[:, None, :]
    lower_half = heads[..., :half_width]
    upper_half = heads[..., half_width:]
    return jnp.concatenate([lower_half * cosine - upper_half * sine_term, upper_half * cosine + lower_half * sine_term], axis=-1)

def mask_of(query_doc, query_pos, query_live, key_doc, key_pos, key_live):
    return (query_doc[:, None] == key_doc[None, :]) & (key_pos[None, :] <= query_pos[:, None]) & query_live[:, None] & key_live[None, :]

def attend_scores(query_matrix, key_heads, score_scale):
    return jnp.einsum('bkgd,mkd->kgbm', query_matrix.astype(jnp.float32), key_heads.astype(jnp.float32)) * score_scale

def attend_forward(query_matrix, key_heads, value_heads, allowed, score_scale):
    scores = attend_scores(query_matrix, key_heads, score_scale)
    row_max = lax.optimization_barrier(jnp.max(jnp.where(allowed, scores, fill_value), axis=-1))
    exponent = jnp.where(allowed, jnp.exp(scores - row_max[..., None]), 0.0)
    row_sum = lax.optimization_barrier(jnp.sum(exponent, axis=-1))
    row_sum = jnp.where(jnp.any(allowed, axis=-1), row_sum, 1.0)
    probability = (exponent / row_sum[..., None]).astype(jnp.bfloat16)
    attended_output = jnp.einsum('kgbm,mkd->bkgd', probability.astype(jnp.float32), value_heads.astype(jnp.float32))
    return (attended_output.astype(jnp.bfloat16), row_max, row_sum)

def attend_backward(query_matrix, key_heads, value_heads, out_grads, attended_output, row_max, row_sum, allowed, score_scale):
    scores = attend_scores(query_matrix, key_heads, score_scale)
    probability = jnp.where(allowed, jnp.exp(scores - row_max[..., None]), 0.0) / row_sum[..., None]
    rounded = probability.astype(jnp.bfloat16)
    row_delta = jnp.einsum('bkgd,bkgd->kgb', out_grads.astype(jnp.float32), attended_output.astype(jnp.float32))
    prob_grad = jnp.einsum('bkgd,mkd->kgbm', out_grads.astype(jnp.float32), value_heads.astype(jnp.float32))
    score_grad = (probability * (prob_grad - row_delta[..., None])).astype(jnp.bfloat16)
    query_gradient = jnp.einsum('kgbm,mkd->bkgd', score_grad.astype(jnp.float32), key_heads.astype(jnp.float32)) * score_scale
    key_gradient = jnp.einsum('kgbm,bkgd->mkd', score_grad.astype(jnp.float32), query_matrix.astype(jnp.float32)) * score_scale
    value_gradient = jnp.einsum('kgbm,bkgd->mkd', rounded.astype(jnp.float32), out_grads.astype(jnp.float32))
    return (query_gradient, key_gradient, value_gradient)

def reference(normed_input, w_query, key_weight, value_weight, output_weight, output_cotangent, piece_doc, piece_offset, doc_owner):
    token_list = normed_input.shape[0]
    group_width = QUERY_HEAD_COUNT // KV_HEAD_COUNT
    score_scale = 1.0 / math.sqrt(HEAD_SIZE)
    within = jnp.arange(PIECE, dtype=jnp.int32)
    token_doc = jnp.repeat(piece_doc, PIECE)
    token_position = (piece_offset[:, None] + within[None, :]).reshape(-1)
    token_owner = doc_owner[token_doc]
    owner_order = jnp.argsort(token_owner, stable=True).astype(jnp.int32).reshape(N_CTX, TOKENS_PER_SHARD)
    query_row_block = apply_rotary(jnp.dot(normed_input, w_query, preferred_element_type=jnp.float32).reshape(token_list, QUERY_HEAD_COUNT, HEAD_SIZE), token_position, 1.0).astype(jnp.bfloat16)
    key_row_block = apply_rotary(jnp.dot(normed_input, key_weight, preferred_element_type=jnp.float32).reshape(token_list, KV_HEAD_COUNT, HEAD_SIZE), token_position, 1.0).astype(jnp.bfloat16)
    value_row_block = jnp.dot(normed_input, value_weight, preferred_element_type=jnp.float32).astype(jnp.bfloat16).reshape(token_list, KV_HEAD_COUNT, HEAD_SIZE)
    head_gradient = jnp.dot(output_cotangent, output_weight, preferred_element_type=jnp.float32).astype(jnp.bfloat16).reshape(token_list, KV_HEAD_COUNT, group_width, HEAD_SIZE)

    def per_owner(group_members):
        query_matrix = query_row_block[group_members].reshape(TOKENS_PER_SHARD, KV_HEAD_COUNT, group_width, HEAD_SIZE)
        key_heads = key_row_block[group_members]
        value_heads = value_row_block[group_members]
        out_grads = head_gradient[group_members]
        docs = token_doc[group_members]
        positions = token_position[group_members]
        live_rows = jnp.ones((TOKENS_PER_SHARD,), dtype=bool)
        allowed = mask_of(docs, positions, live_rows, docs, positions, live_rows)
        attended_output, row_max, row_sum = attend_forward(query_matrix, key_heads, value_heads, allowed, score_scale)
        query_gradient, key_gradient, value_gradient = attend_backward(query_matrix, key_heads, value_heads, out_grads, attended_output, row_max, row_sum, allowed, score_scale)
        query_gradient = apply_rotary(query_gradient.reshape(TOKENS_PER_SHARD, QUERY_HEAD_COUNT, HEAD_SIZE), positions, -1.0).astype(jnp.bfloat16)
        key_gradient = apply_rotary(key_gradient, positions, -1.0).astype(jnp.bfloat16)
        return (attended_output.reshape(TOKENS_PER_SHARD, QUERY_HEAD_COUNT * HEAD_SIZE), query_gradient.reshape(TOKENS_PER_SHARD, QUERY_HEAD_COUNT * HEAD_SIZE), key_gradient.reshape(TOKENS_PER_SHARD, KV_HEAD_COUNT * HEAD_SIZE), value_gradient.astype(jnp.bfloat16).reshape(TOKENS_PER_SHARD, KV_HEAD_COUNT * HEAD_SIZE))
    outputs = lax.map(per_owner, owner_order)
    flat_order = owner_order.reshape(-1)

    def place(stacked):
        return jnp.zeros((token_list, stacked.shape[-1]), stacked.dtype).at[flat_order].set(stacked.reshape(token_list, -1))
    attended_output = place(outputs[0])
    query_gradient = place(outputs[1])
    key_gradient = place(outputs[2])
    value_gradient = place(outputs[3])
    grad_in = (jnp.dot(query_gradient, w_query.T, preferred_element_type=jnp.float32) + jnp.dot(key_gradient, key_weight.T, preferred_element_type=jnp.float32) + jnp.dot(value_gradient, value_weight.T, preferred_element_type=jnp.float32)).astype(jnp.bfloat16)
    grad_query = jnp.dot(normed_input.T, query_gradient, preferred_element_type=jnp.float32).astype(jnp.bfloat16)
    grad_key = jnp.dot(normed_input.T, key_gradient, preferred_element_type=jnp.float32).astype(jnp.bfloat16)
    grad_value = jnp.dot(normed_input.T, value_gradient, preferred_element_type=jnp.float32).astype(jnp.bfloat16)
    grad_out = jnp.dot(output_cotangent.T, attended_output, preferred_element_type=jnp.float32).astype(jnp.bfloat16)
    return (grad_in, grad_query, grad_key, grad_value, grad_out)
```

```python
import functools
import math

import jax
import jax.numpy as jnp
from jax import lax
from jax.experimental import pallas as pl
from jax.experimental.pallas import tpu as pltpu
from jax.sharding import Mesh, PartitionSpec as P

HEAD = 128
PIECE = 8
ROPE_BASE = 500000.0
FILL = -1e30
NX, NZ, NC, NT = 4, 4, 2, 4
CTX = ("x", "z", "c")
N_CTX = NX * NZ * NC
TOK = 512
WIDTH = 4096
QW = 512
KW = 128
COLS = 1280
K0, V0, G0 = 512, 640, 768
PAIR = 32
TARGETS = 16
PIECES = TOK // PIECE
MAX_POS = 512
SCALE = 1.0 / math.sqrt(HEAD)
BF = jnp.bfloat16
F32 = jnp.float32
NN = (((1,), (0,)), ((), ()))
NTD = (((1,), (1,)), ((), ()))
TN = (((0,), (0,)), ((), ()))


def dot(a, b, dims=NN):
    return lax.dot_general(a, b, dims, preferred_element_type=F32)


def vmem_spec():
    return pl.BlockSpec(memory_space=pltpu.VMEM)


def params(**kw):
    return pltpu.CompilerParams(vmem_limit_bytes=56 * 1024 * 1024, **kw)


def cost(flops, nbytes):
    return pl.CostEstimate(flops=int(flops), bytes_accessed=int(nbytes), transcendentals=0)


def rotary_tables():
    half = HEAD // 2
    frequency = ROPE_BASE ** (-2.0 * jnp.arange(half, dtype=F32) / HEAD)
    angles = jnp.arange(MAX_POS, dtype=F32)[:, None] * frequency[None, :]
    cosine, sine = jnp.cos(angles), jnp.sin(angles)
    return (
        jnp.concatenate([cosine, cosine], axis=1),
        jnp.concatenate([-sine, sine], axis=1),
    )


def gather_tables(offsets, cos_table, sin_table, cos_rows, sin_rows):
    for i in range(PIECES):
        at = pl.multiple_of(offsets[i], PIECE)
        cos_rows[i * PIECE : (i + 1) * PIECE, :] = cos_table[pl.ds(at, PIECE), :]
        sin_rows[i * PIECE : (i + 1) * PIECE, :] = sin_table[pl.ds(at, PIECE), :]


def project_kernel(
    places,
    offsets,
    targets,
    x_ref,
    c_ref,
    wq_ref,
    wk_ref,
    wv_ref,
    wo_ref,
    rows_ref,
    cos_table,
    sin_table,
    out_ref,
    xk_ref,
    xs_ref,
    ck_ref,
    cs_ref,
    acc,
    cos_rows,
    sin_rows,
):
    step = pl.program_id(0)
    core = places[8]

    @pl.when(step == 0)
    def _():
        acc[...] = jnp.zeros_like(acc)

    x = x_ref[...]
    acc[:, :K0] += dot(x, wq_ref[...])
    acc[:, K0:V0] += dot(x, wk_ref[...])
    acc[:, V0:G0] += dot(x, wv_ref[...])
    acc[:, G0:] += dot(c_ref[...], wo_ref[...])
    for i in range(NZ):
        base = places[4 + i] * 2
        keep = pl.ds(pl.multiple_of((base + core) * HEAD, HEAD), HEAD)
        send = pl.ds(pl.multiple_of((base + 1 - core) * HEAD, HEAD), HEAD)
        put = slice(i * HEAD, (i + 1) * HEAD)
        xk_ref[:, put] = x_ref[:, keep]
        xs_ref[:, put] = x_ref[:, send]
        ck_ref[:, put] = c_ref[:, keep]
        cs_ref[:, put] = c_ref[:, send]

    @pl.when(step == pl.num_programs(0) - 1)
    def _():
        gather_tables(offsets, cos_table, sin_table, cos_rows, sin_rows)
        cosine, sine = cos_rows[...], sin_rows[...]
        parts = []
        for h in range(5):
            u = acc[:, h * HEAD : (h + 1) * HEAD]
            parts.append((u * cosine + pltpu.roll(u, HEAD // 2, 1) * sine).astype(BF))
        parts.append(acc[:, V0:].astype(BF))
        tokens = jnp.concatenate(parts, axis=1)
        slot = lax.broadcasted_iota(jnp.int32, (TOK, TOK), 0)
        one_hot = jnp.where(slot == rows_ref[...], 1.0, 0.0).astype(BF)
        packed = dot(one_hot, tokens).astype(BF)
        for k in range(TARGETS):
            out_ref[targets[k]] = packed[k * PAIR : (k + 1) * PAIR, :]


def project(places, offsets, targets, x, c, wq, wk, wv, wo, rows, cos_table, sin_table):
    steps = NX
    depth = WIDTH // steps
    column = lambda i, *_: (0, i)
    row = lambda i, *_: (i, 0)
    fixed = lambda i, *_: (0, 0)
    rolled = lambda i, places, *_: (0, places[i])
    half = jax.ShapeDtypeStruct((TOK, WIDTH // 2), BF)
    return pl.pallas_call(
        project_kernel,
        grid_spec=pltpu.PrefetchScalarGridSpec(
            num_scalar_prefetch=3,
            grid=(steps,),
            in_specs=[
                pl.BlockSpec((TOK, depth), column),
                pl.BlockSpec((TOK, depth), column),
                pl.BlockSpec((depth, QW), row),
                pl.BlockSpec((depth, KW), row),
                pl.BlockSpec((depth, KW), row),
                pl.BlockSpec((depth, QW), row),
                pl.BlockSpec((1, TOK), fixed),
                pl.BlockSpec((MAX_POS, HEAD), fixed),
                pl.BlockSpec((MAX_POS, HEAD), fixed),
            ],
            out_specs=[pl.BlockSpec((N_CTX, PAIR, COLS), lambda i, *_: (0, 0, 0))]
            + [pl.BlockSpec((TOK, depth // 2), rolled)] * 4,
            scratch_shapes=[
                pltpu.VMEM((TOK, COLS), F32),
                pltpu.VMEM((TOK, HEAD), F32),
                pltpu.VMEM((TOK, HEAD), F32),
            ],
        ),
        out_shape=[jax.ShapeDtypeStruct((N_CTX, PAIR, COLS), BF)] + [half] * 4,
        compiler_params=params(),
        cost_estimate=cost(6e9, 28e6),
        name="project",
    )(places, offsets, targets, x, c, wq, wk, wv, wo, rows, cos_table, sin_table)


def attend_kernel(
    live,
    offsets,
    got_ref,
    cos_table,
    sin_table,
    doc_col,
    doc_row,
    pos_col,
    pos_row,
    out_ref,
    rows,
    back,
    bias,
    cos_rows,
    sin_rows,
):
    gather_tables(offsets, cos_table, sin_table, cos_rows, sin_rows)
    for k in range(TARGETS):
        rows[k * PAIR : (k + 1) * PAIR, :] = got_ref[live[k]]
    allowed = (doc_col[...] == doc_row[...]) & (pos_row[...] <= pos_col[...])
    bias[...] = jnp.where(allowed, 0.0, FILL)
    keys = rows[:, K0:V0]
    values = rows[:, V0:G0]
    key_grad = jnp.zeros((TOK, HEAD), F32)
    value_grad = jnp.zeros((TOK, HEAD), F32)
    half = HEAD // 2

    def unrotate(u):
        return u * cos_rows[...] - pltpu.roll(u, half, 1) * sin_rows[...]

    for h in range(QW // HEAD):
        here = slice(h * HEAD, (h + 1) * HEAD)
        there = slice(G0 + h * HEAD, G0 + (h + 1) * HEAD)
        query = rows[:, here]
        grads = rows[:, there]
        scores = dot(query, keys, NTD) * SCALE + bias[...]
        weight = jnp.exp(scores - jnp.max(scores, axis=1, keepdims=True))
        prob = weight * (1.0 / jnp.sum(weight, axis=1, keepdims=True))
        rounded = prob.astype(BF)
        attended = dot(rounded, values).astype(BF)
        back[:, there] = attended
        delta = jnp.sum(grads.astype(F32) * attended.astype(F32), axis=1, keepdims=True)
        prob_grad = dot(grads, values, NTD)
        score_grad = (prob * (prob_grad - delta)).astype(BF)
        back[:, here] = unrotate(dot(score_grad, keys) * SCALE).astype(BF)
        key_grad = key_grad + dot(score_grad, query, TN)
        value_grad = value_grad + dot(rounded, grads, TN)
    back[:, K0:V0] = unrotate(key_grad * SCALE).astype(BF)
    back[:, V0:G0] = value_grad.astype(BF)
    for k in range(TARGETS):
        out_ref[live[k]] = back[k * PAIR : (k + 1) * PAIR, :]


def attend(live, offsets, got, cos_table, sin_table, doc_col, doc_row, pos_col, pos_row):
    return pl.pallas_call(
        attend_kernel,
        in_specs=[pl.BlockSpec(memory_space=pltpu.SMEM)] * 2 + [vmem_spec()] * 7,
        out_specs=vmem_spec(),
        out_shape=jax.ShapeDtypeStruct((N_CTX, PAIR, COLS), BF),
        scratch_shapes=[
            pltpu.VMEM((TOK, COLS), BF),
            pltpu.VMEM((TOK, COLS), BF),
            pltpu.VMEM((TOK, TOK), F32),
            pltpu.VMEM((TOK, HEAD), F32),
            pltpu.VMEM((TOK, HEAD), F32),
        ],
        compiler_params=params(),
        cost_estimate=cost(4e9, 6e6),
        name="attend",
    )(live, offsets, got, cos_table, sin_table, doc_col, doc_row, pos_col, pos_row)


def restore_kernel(targets, got_ref, rows_ref, out_ref, turned_ref, packed):
    for k in range(TARGETS):
        packed[k * PAIR : (k + 1) * PAIR, :] = got_ref[targets[k]]
    slot = lax.broadcasted_iota(jnp.int32, (TOK, TOK), 0)
    one_hot = jnp.where(slot == rows_ref[...], 1.0, 0.0).astype(BF)
    tokens = dot(one_hot, packed[...], TN).astype(BF)
    out_ref[...] = tokens
    turned_ref[...] = tokens.T


def restore(targets, got, rows):
    return pl.pallas_call(
        restore_kernel,
        in_specs=[pl.BlockSpec(memory_space=pltpu.SMEM), vmem_spec(), vmem_spec()],
        out_specs=[vmem_spec(), vmem_spec()],
        out_shape=[
            jax.ShapeDtypeStruct((TOK, COLS), BF),
            jax.ShapeDtypeStruct((COLS, TOK), BF),
        ],
        scratch_shapes=[pltpu.VMEM((TOK, COLS), BF)],
        compiler_params=params(),
        cost_estimate=cost(1e9, 6e6),
        name="restore",
    )(targets, got, rows)


def input_grad_kernel(count, split, where, dy_ref, wq_ref, wk_ref, wv_ref, *outs):
    total = (
        dot(dy_ref[:, :K0], wq_ref[...], NTD)
        + dot(dy_ref[:, K0:V0], wk_ref[...], NTD)
        + dot(dy_ref[:, V0:G0], wv_ref[...], NTD)
    )
    if split:
        outs[0][...] = total[: TOK // 2].astype(BF)
        outs[1][...] = total[TOK // 2 :].astype(BF)
    else:
        outs[0][...] = total


def input_grad(where, at, count, split, dy, wq, wk, wv):
    span = WIDTH // NT
    block = lambda i, where: (where[at + i], 0)
    if split:
        half = jax.ShapeDtypeStruct((TOK // 2, span), BF)
        out_shape = [half, half]
        out_specs = [pl.BlockSpec((TOK // 2, span), lambda i, *_: (0, 0))] * 2
    else:
        out_shape = [jax.ShapeDtypeStruct((count * TOK, span), F32)]
        out_specs = [pl.BlockSpec((TOK, span), lambda i, *_: (i, 0))]
    return pl.pallas_call(
        functools.partial(input_grad_kernel, count, split),
        grid_spec=pltpu.PrefetchScalarGridSpec(
            num_scalar_prefetch=1,
            grid=(count,),
            in_specs=[
                pl.BlockSpec((TOK, COLS), lambda i, *_: (0, 0)),
                pl.BlockSpec((span, QW), block),
                pl.BlockSpec((span, KW), block),
                pl.BlockSpec((span, KW), block),
            ],
            out_specs=out_specs,
        ),
        out_shape=out_shape,
        compiler_params=params(),
        cost_estimate=cost(0.8e9 * count, 5e6 * count),
        name="input_grad",
    )(where, dy, wq, wk, wv)


HALF = 640


def weight_grad_kernel(
    split, own, peer, xa0, xa1, c0, c1, b00, b01, b02, b03, b10, b11, b12, b13, *outs
):
    first = dot(own[V0:G0, :], xa0[...]) + dot(peer[V0:G0, :], xa1[...])
    second = dot(own[G0:, :], c0[...]) + dot(peer[G0:, :], c1[...])
    xb0 = jnp.concatenate([b00[...], b01[...], b02[...], b03[...]], axis=1)
    xb1 = jnp.concatenate([b10[...], b11[...], b12[...], b13[...]], axis=1)
    third = dot(own[:V0, :], xb0) + dot(peer[:V0, :], xb1)
    cut = HALF // 2
    if split:
        a0, a1, b0, b1 = outs
        a0[:KW, :] = first.astype(BF)
        a0[KW:, :] = second[: cut - KW].astype(BF)
        a1[...] = second[cut - KW :].astype(BF)
        b0[...] = third[:cut].astype(BF)
        b1[...] = third[cut:].astype(BF)
    else:
        a, b = outs
        a[:KW, :] = first
        a[KW:, :] = second
        b[...] = third


def weight_grad(at, count, split, own, peer, xk, xr, ck, cr):
    wide = NZ * HEAD
    whole = lambda i: (0, 0)
    block = lambda i: (0, at + i)
    spec_a = pl.BlockSpec((TOK, wide), block)
    specs_b = [
        pl.BlockSpec((TOK, HEAD), functools.partial(lambda j, i: (0, j * NZ + at + i), j))
        for j in range(NX)
    ]
    if split:
        shape = jax.ShapeDtypeStruct((HALF // 2, wide), BF)
        out_shape = [shape] * 4
        out_specs = [pl.BlockSpec((HALF // 2, wide), whole)] * 4
    else:
        shape = jax.ShapeDtypeStruct((count * HALF, wide), F32)
        out_shape = [shape] * 2
        out_specs = [pl.BlockSpec((HALF, wide), lambda i: (i, 0))] * 2
    return pl.pallas_call(
        functools.partial(weight_grad_kernel, split),
        grid=(count,),
        in_specs=[
            pl.BlockSpec((COLS, TOK), whole),
            pl.BlockSpec((COLS, TOK), whole),
            spec_a,
            spec_a,
            spec_a,
            spec_a,
        ]
        + specs_b
        + specs_b,
        out_specs=out_specs,
        out_shape=out_shape,
        compiler_params=params(),
        cost_estimate=cost(1.4e9 * count, 6e6 * count),
        name="weight_grad",
    )(own, peer, xk, xr, ck, cr, xk, xk, xk, xk, xr, xr, xr, xr)


def shift(value, axis, by):
    n = lax.axis_size(axis)
    return lax.ppermute(value, axis, [(i, (i + by) % n) for i in range(n)])


def pass_far(up_half, down_half, axis):
    return shift(up_half, axis, 1), shift(down_half, axis, -1)


def pass_near(up, down, from_below, from_above, axis):
    cut = up.shape[0] // 2
    up = jnp.concatenate([up[:cut] + from_below.astype(F32), up[cut:]], axis=0).astype(BF)
    down = jnp.concatenate([down[:cut], down[cut:] + from_above.astype(F32)], axis=0).astype(BF)
    return shift(up, axis, 1), shift(down, axis, -1)


def total_of(own, near):
    return own + near[0].astype(F32) + near[1].astype(F32)


def finish_ring(total, axis):
    cut = total.shape[0] // 2
    far = total[:, :HEAD].astype(BF)
    halves = pass_far(far[:cut], far[cut:], axis)
    near = pass_near(total[:, HEAD : 2 * HEAD], total[:, 2 * HEAD : 3 * HEAD], *halves, axis)
    return total_of(total[:, 3 * HEAD :], near)


def on_device(x, wq, wk, wv, wo, c, piece_doc, piece_offset, doc_owner):
    ix, iz, ic, iy = (lax.axis_index(a) for a in ("x", "z", "c", "tp"))
    me = (ix * NZ + iz) * NC + ic
    i32 = jnp.int32
    relative = jnp.array([2, 1, 3, 0], i32)
    x_dest = (ix + relative) % NX
    z_dest = (iz + relative) % NZ
    y_dest = (iy + relative) % NT
    x_rank = jnp.array([3, 1, 0, 2], i32)[(jnp.arange(NX, dtype=i32) - ix) % NX]
    places = jnp.concatenate([x_rank, z_dest, ic[None].astype(i32)])

    doc_grid = piece_doc.reshape(N_CTX, PIECES)
    offset_grid = piece_offset.reshape(N_CTX, PIECES)
    own_doc = lax.dynamic_slice_in_dim(piece_doc, me * PIECES, PIECES)
    own_offset = lax.dynamic_slice_in_dim(piece_offset, me * PIECES, PIECES)
    doc_ids = jnp.arange(doc_owner.shape[0], dtype=i32)
    own_owner = jnp.sum(jnp.where(own_doc[:, None] == doc_ids[None, :], doc_owner[None, :], 0), axis=1)
    ids = jnp.arange(PIECES, dtype=i32)
    order_key = own_owner * PIECES + ids
    slot = jnp.sum((order_key[None, :] < order_key[:, None]).astype(i32), axis=1)
    blocks = jnp.arange(TARGETS, dtype=i32) * (PAIR // PIECE)
    targets = jnp.sum(jnp.where(blocks[:, None] == slot[None, :], own_owner[None, :], 0), axis=1)
    within = jnp.arange(PIECE, dtype=i32)
    packed_row = (slot[:, None] * PIECE + within[None, :]).reshape(1, TOK)

    mine_doc = doc_owner == me
    doc_rank = jnp.sum((mine_doc[None, :] & (doc_ids[None, :] < doc_ids[:, None])).astype(i32), axis=1)
    four = jnp.arange(4, dtype=i32)
    my_docs = jnp.sum(
        jnp.where(mine_doc[None, :] & (doc_rank[None, :] == four[:, None]), doc_ids[None, :], 0), axis=1
    )
    mine = jnp.any(doc_grid[None, :, :] == my_docs[:, None, None], axis=0)
    before = (ids[:, None] < ids[None, :]).astype(BF)
    rank_in = jnp.dot(mine.astype(BF), before, preferred_element_type=F32).astype(i32)
    is_live = jnp.any(mine, axis=1)
    sources = jnp.arange(N_CTX, dtype=i32)
    live_rank = jnp.sum((is_live[None, :] & (sources[None, :] < sources[:, None])).astype(i32), axis=1)
    kth = jnp.arange(TARGETS, dtype=i32)
    live = jnp.sum(
        jnp.where(is_live[None, :] & (live_rank[None, :] == kth[:, None]), sources[None, :], 0), axis=1
    )
    index = jnp.where(mine, live_rank[:, None] * (PAIR // PIECE) + rank_in, -1).reshape(1, -1)
    chosen = index == ids[:, None]
    live_doc = jnp.sum(jnp.where(chosen, piece_doc[None, :], 0), axis=1)
    live_offset = jnp.sum(jnp.where(chosen, piece_offset[None, :], 0), axis=1)
    row_doc = jnp.repeat(live_doc, PIECE)
    row_pos = (live_offset[:, None] + within[None, :]).reshape(-1)

    cos_table, sin_table = rotary_tables()
    sent, xk, xs, ck, cs = project(
        places, own_offset, targets, x, c, wq, wk, wv, wo, packed_row, cos_table, sin_table
    )
    xr = shift(xs, "c", 1)
    cr = shift(cs, "c", 1)
    got = lax.all_to_all(sent, CTX, split_axis=0, concat_axis=0, tiled=True)
    back = attend(
        live,
        live_offset,
        got,
        cos_table,
        sin_table,
        row_doc[:, None],
        row_doc[None, :],
        row_pos[:, None],
        row_pos[None, :],
    )
    home = lax.all_to_all(back, CTX, split_axis=0, concat_axis=0, tiled=True)
    dy, own = restore(targets, home, packed_row)
    peer = shift(own, "c", 1)

    far = input_grad(y_dest, 0, 1, True, dy, wq, wk, wv)
    y_far = pass_far(*far, "tp")
    a0, a1, b0, b1 = weight_grad(0, 1, True, own, peer, xk, xr, ck, cr)
    a_far = pass_far(a0, a1, "x")
    b_far = pass_far(b0, b1, "z")
    (near,) = input_grad(y_dest, 1, 2, False, dy, wq, wk, wv)
    a_near, b_near = weight_grad(1, 2, False, own, peer, xk, xr, ck, cr)
    y_near = pass_near(near[:TOK], near[TOK:], *y_far, "tp")
    a_near = pass_near(a_near[:HALF], a_near[HALF:], *a_far, "x")
    b_near = pass_near(b_near[:HALF], b_near[HALF:], *b_far, "z")
    (y_own,) = input_grad(y_dest, 3, 1, False, dy, wq, wk, wv)
    a_own, b_own = weight_grad(3, 1, False, own, peer, xk, xr, ck, cr)
    a = finish_ring(total_of(a_own, a_near), "z")
    b = finish_ring(total_of(b_own, b_near), "x")
    grad_in = total_of(y_own, y_near).astype(BF)
    grad_query = b[:QW].T.astype(BF)
    grad_key = b[QW:].T.astype(BF)
    grad_value = a[:KW].T.astype(BF)
    grad_out = a[KW:].T.astype(BF)
    return grad_in, grad_query, grad_key, grad_value, grad_out


def solution(mesh):
    fine = Mesh(mesh.devices.reshape(NX, NZ, NC, NT), ("x", "z", "c", "tp"))
    column = P(None, "tp")
    both = P(CTX, "tp")
    return jax.shard_map(
        on_device,
        mesh=fine,
        in_specs=(P(CTX, None), column, column, column, column, P(CTX, None), P(), P(), P()),
        out_specs=(both,) * 5,
        check_vma=False,
    )
```

```python
import functools
import math

import jax
import jax.numpy as jnp
import numpy as np
from jax import lax
from jax.experimental import pallas as pl
from jax.experimental.pallas import tpu as pltpu
from jax.sharding import Mesh, PartitionSpec as P

HEAD = 128
PIECE = 8
ROPE_BASE = 500000.0
FILL = -1e30
NX, NZ, NC, NT = 4, 4, 2, 4
CTX = ("x", "z", "c")
N_CTX = NX * NZ * NC
TOK = 512
WIDTH = 4096
QW = 512
KW = 128
COLS = 1280
K0, V0, G0 = 512, 640, 768
PAIR = 32
TARGETS = 16
PIECES = TOK // PIECE
MAX_POS = 512
HALF = 640
CUT = HALF // 2
FAR, UP, OWN, DOWN = 0, 1, 2, 3
SCALE = 1.0 / math.sqrt(HEAD)
BF = jnp.bfloat16
F32 = jnp.float32
I32 = jnp.int32
NN = (((1,), (0,)), ((), ()))
NTD = (((1,), (1,)), ((), ()))
TN = (((0,), (0,)), ((), ()))


def dot(a, b, dims=NN):
    return lax.dot_general(a, b, dims, preferred_element_type=F32)


def vmem_spec():
    return pl.BlockSpec(memory_space=pltpu.VMEM)


def smem_spec():
    return pl.BlockSpec(memory_space=pltpu.SMEM)


def any_spec():
    return pl.BlockSpec(memory_space=pl.ANY)


def params(mib):
    return pltpu.CompilerParams(vmem_limit_bytes=mib * 1024 * 1024)


def cost(flops, nbytes):
    return pl.CostEstimate(flops=int(flops), bytes_accessed=int(nbytes), transcendentals=0)


def rotary_tables():
    half = HEAD // 2
    frequency = np.float32(ROPE_BASE) ** (-2.0 * np.arange(half, dtype=np.float32) / np.float32(HEAD))
    angles = np.arange(MAX_POS, dtype=np.float32)[:, None] * frequency.astype(np.float32)[None, :]
    cosine, sine = np.cos(angles), np.sin(angles)
    return (
        jnp.asarray(np.concatenate([cosine, cosine], axis=1).astype(np.float32)),
        jnp.asarray(np.concatenate([-sine, sine], axis=1).astype(np.float32)),
    )


def related(coordinate, order):
    return (coordinate + 2 - order) & 3


def project_kernel(
    me,
    piece_doc,
    piece_offset,
    doc_owner,
    x_ref,
    c_ref,
    wq_ref,
    wk_ref,
    wv_ref,
    wo_ref,
    cos_table,
    sin_table,
    out_ref,
    acc,
    packed,
    owner_of,
    rank_of,
    count,
    first,
    targets,
):
    step = pl.program_id(0)
    steps = pl.num_programs(0)
    each = PIECES // (WIDTH // 512)

    @pl.when(step == 0)
    def _():
        acc[...] = jnp.zeros_like(acc)
        for o in range(N_CTX):
            count[o] = 0

    for j in range(each):
        i = step * each + j
        owner = doc_owner[piece_doc[me[0] * PIECES + i]]
        owner_of[i] = owner
        rank_of[i] = count[owner]
        count[owner] = count[owner] + 1
    x = x_ref[...]
    acc[:, :K0] += dot(x, wq_ref[...])
    acc[:, K0:V0] += dot(x, wk_ref[...])
    acc[:, V0:G0] += dot(x, wv_ref[...])
    acc[:, G0:] += dot(c_ref[...], wo_ref[...])

    @pl.when(step == steps - 1)
    def _():
        run = jnp.int32(0)
        for o in range(N_CTX):
            first[o] = run
            targets[run >> 2] = jnp.int32(o)
            run = run + count[o]
        for i in range(PIECES):
            at = pl.multiple_of(piece_offset[me[0] * PIECES + i], PIECE)
            to = pl.multiple_of((first[owner_of[i]] + rank_of[i]) * PIECE, PIECE)
            here = slice(i * PIECE, (i + 1) * PIECE)
            cosine = cos_table[pl.ds(at, PIECE), :]
            sine = sin_table[pl.ds(at, PIECE), :]
            for h in range(5):
                span = slice(h * HEAD, (h + 1) * HEAD)
                u = acc[here, span]
                packed[pl.ds(to, PIECE), span] = u * cosine + pltpu.roll(u, HEAD // 2, 1) * sine
            packed[pl.ds(to, PIECE), V0:] = acc[here, V0:]
        for k in range(TARGETS):
            out_ref[targets[k]] = packed[k * PAIR : (k + 1) * PAIR, :].astype(BF)


def project(me, piece_doc, piece_offset, doc_owner, x, c, wq, wk, wv, wo, cos_table, sin_table):
    depth = 512
    column = lambda i, *_: (0, i)
    row = lambda i, *_: (i, 0)
    fixed = lambda i, *_: (0, 0)
    smem = pltpu.SMEM
    return pl.pallas_call(
        project_kernel,
        grid_spec=pltpu.PrefetchScalarGridSpec(
            num_scalar_prefetch=4,
            grid=(WIDTH // depth,),
            in_specs=[
                pl.BlockSpec((TOK, depth), column),
                pl.BlockSpec((TOK, depth), column),
                pl.BlockSpec((depth, QW), row),
                pl.BlockSpec((depth, KW), row),
                pl.BlockSpec((depth, KW), row),
                pl.BlockSpec((depth, QW), row),
                pl.BlockSpec((MAX_POS, HEAD), fixed),
                pl.BlockSpec((MAX_POS, HEAD), fixed),
            ],
            out_specs=pl.BlockSpec((N_CTX, PAIR, COLS), lambda i, *_: (0, 0, 0)),
            scratch_shapes=[
                pltpu.VMEM((TOK, COLS), F32),
                pltpu.VMEM((TOK, COLS), F32),
                smem((PIECES,), I32),
                smem((PIECES,), I32),
                smem((N_CTX,), I32),
                smem((N_CTX,), I32),
                smem((N_CTX,), I32),
            ],
        ),
        out_shape=jax.ShapeDtypeStruct((N_CTX, PAIR, COLS), BF),
        compiler_params=params(60),
        cost_estimate=cost(6e9, 24e6),
        name="project",
    )(me, piece_doc, piece_offset, doc_owner, x, c, wq, wk, wv, wo, cos_table, sin_table)


def regroup_kernel(where, after, x_ref, c_ref, xk_ref, xs_ref, ck_ref, cs_ref):
    core = where[2]
    for i in range(NZ):
        base = related(where[1], i) * 2
        keep = pl.ds(pl.multiple_of((base + core) * HEAD, HEAD), HEAD)
        send = pl.ds(pl.multiple_of((base + 1 - core) * HEAD, HEAD), HEAD)
        xk_ref[i] = x_ref[:, keep]
        xs_ref[i] = x_ref[:, send]
        ck_ref[i] = c_ref[:, keep]
        cs_ref[i] = c_ref[:, send]


def regroup(where, after, x, c):
    part = pl.BlockSpec((TOK, WIDTH // NX), lambda i, where: (0, related(where[0], i)))
    half = jax.ShapeDtypeStruct((NX * NZ, TOK, HEAD), BF)
    return pl.pallas_call(
        regroup_kernel,
        grid_spec=pltpu.PrefetchScalarGridSpec(
            num_scalar_prefetch=1,
            grid=(NX,),
            in_specs=[any_spec(), part, part],
            out_specs=[pl.BlockSpec((NZ, TOK, HEAD), lambda i, where: (i, 0, 0))] * 4,
        ),
        out_shape=[half] * 4,
        compiler_params=params(16),
        cost_estimate=cost(1, 17e6),
        name="regroup",
    )(where, after, x, c)


def fetch_blocks(source, which, rows, sems):
    copies = [
        pltpu.make_async_copy(source.at[which[k]], rows.at[pl.ds(k * PAIR, PAIR)], sems.at[k])
        for k in range(TARGETS)
    ]
    for copy in copies:
        copy.start()
    return copies


def attend_kernel(
    live,
    offsets,
    got_ref,
    cos_table,
    sin_table,
    doc_col,
    doc_row,
    pos_col,
    pos_row,
    out_ref,
    rows,
    back,
    bias,
    cos_rows,
    sin_rows,
    sems,
):
    copies = fetch_blocks(got_ref, live, rows, sems)
    for i in range(PIECES):
        at = pl.multiple_of(offsets[i], PIECE)
        cos_rows[i * PIECE : (i + 1) * PIECE, :] = cos_table[pl.ds(at, PIECE), :]
        sin_rows[i * PIECE : (i + 1) * PIECE, :] = sin_table[pl.ds(at, PIECE), :]
    allowed = (doc_col[...] == doc_row[...]) & (pos_row[...] <= pos_col[...])
    bias[...] = jnp.where(allowed, 0.0, FILL)
    for copy in copies:
        copy.wait()
    keys = rows[:, K0:V0]
    values = rows[:, V0:G0]
    key_grad = jnp.zeros((TOK, HEAD), F32)
    value_grad = jnp.zeros((TOK, HEAD), F32)
    half = HEAD // 2

    def unrotate(u):
        return u * cos_rows[...] - pltpu.roll(u, half, 1) * sin_rows[...]

    for h in range(QW // HEAD):
        here = slice(h * HEAD, (h + 1) * HEAD)
        there = slice(G0 + h * HEAD, G0 + (h + 1) * HEAD)
        query = rows[:, here]
        grads = rows[:, there]
        scores = dot(query, keys, NTD) * SCALE + bias[...]
        weight = jnp.exp(scores - jnp.max(scores, axis=1, keepdims=True))
        prob = weight * (1.0 / jnp.sum(weight, axis=1, keepdims=True))
        rounded = prob.astype(BF)
        attended = dot(rounded, values).astype(BF)
        back[:, there] = attended
        delta = jnp.sum(grads.astype(F32) * attended.astype(F32), axis=1, keepdims=True)
        prob_grad = dot(grads, values, NTD)
        score_grad = (prob * (prob_grad - delta)).astype(BF)
        back[:, here] = unrotate(dot(score_grad, keys) * SCALE).astype(BF)
        key_grad = key_grad + dot(score_grad, query, TN)
        value_grad = value_grad + dot(rounded, grads, TN)
    back[:, K0:V0] = unrotate(key_grad * SCALE).astype(BF)
    back[:, V0:G0] = value_grad.astype(BF)
    for k in range(TARGETS):
        out_ref[live[k]] = back[k * PAIR : (k + 1) * PAIR, :]


def attend(live, offsets, got, cos_table, sin_table, doc_col, doc_row, pos_col, pos_row):
    return pl.pallas_call(
        attend_kernel,
        in_specs=[smem_spec(), smem_spec(), any_spec()] + [vmem_spec()] * 6,
        out_specs=vmem_spec(),
        out_shape=jax.ShapeDtypeStruct((N_CTX, PAIR, COLS), BF),
        scratch_shapes=[
            pltpu.VMEM((TOK, COLS), BF),
            pltpu.VMEM((TOK, COLS), BF),
            pltpu.VMEM((TOK, TOK), F32),
            pltpu.VMEM((TOK, HEAD), F32),
            pltpu.VMEM((TOK, HEAD), F32),
            pltpu.SemaphoreType.DMA((TARGETS,)),
        ],
        compiler_params=params(28),
        cost_estimate=cost(4e9, 6e6),
        name="attend",
    )(live, offsets, got, cos_table, sin_table, doc_col, doc_row, pos_col, pos_row)


def input_dot(dy, wq_ref, wk_ref, wv_ref):
    return (
        dot(dy[:, :K0], wq_ref[...], NTD)
        + dot(dy[:, K0:V0], wk_ref[...], NTD)
        + dot(dy[:, V0:G0], wv_ref[...], NTD)
    )


def restore_kernel(
    where, targets, got_ref, rows_ref, wq_ref, wk_ref, wv_ref, out_ref, up_ref, down_ref, packed, sems
):
    copies = fetch_blocks(got_ref, targets, packed, sems)
    slot = lax.broadcasted_iota(I32, (TOK, TOK), 0)
    one_hot = jnp.where(slot == rows_ref[...], 1.0, 0.0).astype(BF)
    for copy in copies:
        copy.wait()
    dy = dot(one_hot, packed[...], TN).astype(BF)
    out_ref[...] = dy
    total = input_dot(dy, wq_ref, wk_ref, wv_ref)
    up_ref[...] = total[: TOK // 2].astype(BF)
    down_ref[...] = total[TOK // 2 :].astype(BF)


def restore(where, targets, got, rows, wq, wk, wv):
    span = WIDTH // NT
    block = lambda i, where, targets: (related(where[3], FAR), 0)
    fixed = lambda i, *_: (0, 0)
    half = jax.ShapeDtypeStruct((TOK // 2, span), BF)
    return pl.pallas_call(
        restore_kernel,
        grid_spec=pltpu.PrefetchScalarGridSpec(
            num_scalar_prefetch=2,
            grid=(1,),
            in_specs=[
                any_spec(),
                pl.BlockSpec((1, TOK), fixed),
                pl.BlockSpec((span, QW), block),
                pl.BlockSpec((span, KW), block),
                pl.BlockSpec((span, KW), block),
            ],
            out_specs=[
                pl.BlockSpec((TOK, COLS), fixed),
                pl.BlockSpec((TOK // 2, span), fixed),
                pl.BlockSpec((TOK // 2, span), fixed),
            ],
            scratch_shapes=[pltpu.VMEM((TOK, COLS), BF), pltpu.SemaphoreType.DMA((TARGETS,))],
        ),
        out_shape=[jax.ShapeDtypeStruct((TOK, COLS), BF), half, half],
        compiler_params=params(24),
        cost_estimate=cost(1.5e9, 6e6),
        name="restore",
    )(where, targets, got, rows, wq, wk, wv)


def input_grad_kernel(where, after, dy_ref, wq_ref, wk_ref, wv_ref, out_ref):
    out_ref[...] = input_dot(dy_ref[...], wq_ref, wk_ref, wv_ref).astype(BF)


def input_grad(where, after, at, count, dy, wq, wk, wv):
    span = WIDTH // NT
    block = lambda i, where: (related(where[3], at + 2 * i), 0)
    return pl.pallas_call(
        input_grad_kernel,
        grid_spec=pltpu.PrefetchScalarGridSpec(
            num_scalar_prefetch=1,
            grid=(count,),
            in_specs=[
                any_spec(),
                pl.BlockSpec((TOK, COLS), lambda i, *_: (0, 0)),
                pl.BlockSpec((span, QW), block),
                pl.BlockSpec((span, KW), block),
                pl.BlockSpec((span, KW), block),
            ],
            out_specs=pl.BlockSpec((TOK, span), lambda i, *_: (i, 0)),
        ),
        out_shape=jax.ShapeDtypeStruct((count * TOK, span), BF),
        compiler_params=params(24),
        cost_estimate=cost(0.8e9 * count, 5e6 * count),
        name="input_grad",
    )(where, after, dy, wq, wk, wv)


def weight_grad_kernel(after, own, peer, xa0, xa1, c0, c1, b00, b01, b02, b03, b10, b11, b12, b13, *outs):
    wide = lambda ref: jnp.concatenate([ref[j] for j in range(NZ)], axis=1)
    join = lambda refs: jnp.concatenate([ref[0] for ref in refs], axis=1)
    first = dot(own[:, V0:G0], wide(xa0), TN) + dot(peer[:, V0:G0], wide(xa1), TN)
    second = dot(own[:, G0:], wide(c0), TN) + dot(peer[:, G0:], wide(c1), TN)
    third = dot(own[:, :V0], join([b00, b01, b02, b03]), TN) + dot(
        peer[:, :V0], join([b10, b11, b12, b13]), TN
    )
    if len(outs) == 4:
        a0, a1, b0, b1 = outs
        a0[:KW, :] = first.astype(BF)
        a0[KW:, :] = second[: CUT - KW].astype(BF)
        a1[...] = second[CUT - KW :].astype(BF)
        b0[...] = third[:CUT].astype(BF)
        b1[...] = third[CUT:].astype(BF)
    else:
        a, b = outs
        a[:KW, :] = first.astype(BF)
        a[KW:, :] = second.astype(BF)
        b[...] = third.astype(BF)


def weight_grad(after, at, count, split, own, peer, xk, xr, ck, cr):
    wide = NZ * HEAD
    whole = lambda i: (0, 0)
    spec_a = pl.BlockSpec((NZ, TOK, HEAD), lambda i: (at + 2 * i, 0, 0))
    specs_b = [
        pl.BlockSpec((1, TOK, HEAD), functools.partial(lambda j, i: (j * NZ + at + 2 * i, 0, 0), j))
        for j in range(NX)
    ]
    if split:
        out_shape = [jax.ShapeDtypeStruct((CUT, wide), BF)] * 4
        out_specs = [pl.BlockSpec((CUT, wide), whole)] * 4
    else:
        out_shape = [jax.ShapeDtypeStruct((count * HALF, wide), BF)] * 2
        out_specs = [pl.BlockSpec((HALF, wide), lambda i: (i, 0))] * 2
    return pl.pallas_call(
        weight_grad_kernel,
        grid=(count,),
        in_specs=[any_spec(), pl.BlockSpec((TOK, COLS), whole), pl.BlockSpec((TOK, COLS), whole)]
        + [spec_a] * 4
        + specs_b
        + specs_b,
        out_specs=out_specs,
        out_shape=out_shape,
        compiler_params=params(28),
        cost_estimate=cost(1.4e9 * count, 6e6 * count),
        name="weight_grad",
    )(after, own, peer, xk, xr, ck, cr, xk, xk, xk, xk, xr, xr, xr, xr)


def near_kernel(count, *refs):
    for g in range(count):
        near, below, above = refs[3 * g : 3 * g + 3]
        up, down = refs[3 * count + 2 * g : 3 * count + 2 * g + 2]
        rows = up.shape[0]
        cut = rows // 2
        up[:cut] = (near[:cut].astype(F32) + below[...].astype(F32)).astype(BF)
        up[cut:] = near[cut:rows]
        down[:cut] = near[rows : rows + cut]
        down[cut:] = (near[rows + cut :].astype(F32) + above[...].astype(F32)).astype(BF)


def add_near(*groups):
    flat = [value for group in groups for value in group]
    shapes = []
    for near, _, _ in groups:
        shapes += [jax.ShapeDtypeStruct((near.shape[0] // 2, near.shape[1]), BF)] * 2
    return pl.pallas_call(
        functools.partial(near_kernel, len(groups)),
        in_specs=[vmem_spec()] * len(flat),
        out_specs=[vmem_spec()] * len(shapes),
        out_shape=shapes,
        compiler_params=params(16),
        cost_estimate=cost(1e6, 5e6),
        name="add_near",
    )(*flat)


def total_kernel(own_a, up_a, down_a, own_b, up_b, down_b, *outs):
    for g, (own, up, down) in enumerate(((own_a, up_a, down_a), (own_b, up_b, down_b))):
        far_up, far_down, near, own_ref = outs[4 * g : 4 * g + 4]
        total = own[...].astype(F32) + up[...].astype(F32) + down[...].astype(F32)
        far = total[:, FAR * HEAD : (FAR + 1) * HEAD].astype(BF)
        far_up[...] = far[:CUT]
        far_down[...] = far[CUT:]
        near[:HALF] = total[:, UP * HEAD : (UP + 1) * HEAD].astype(BF)
        near[HALF:] = total[:, DOWN * HEAD : (DOWN + 1) * HEAD].astype(BF)
        own_ref[...] = total[:, OWN * HEAD : (OWN + 1) * HEAD]


def add_total(own_a, near_a, own_b, near_b):
    one = [
        jax.ShapeDtypeStruct((CUT, HEAD), BF),
        jax.ShapeDtypeStruct((CUT, HEAD), BF),
        jax.ShapeDtypeStruct((2 * HALF, HEAD), BF),
        jax.ShapeDtypeStruct((HALF, HEAD), F32),
    ]
    return pl.pallas_call(
        total_kernel,
        in_specs=[vmem_spec()] * 6,
        out_specs=[vmem_spec()] * 8,
        out_shape=one + one,
        compiler_params=params(16),
        cost_estimate=cost(1e6, 5e6),
        name="add_total",
    )(own_a, *near_a, own_b, *near_b)


def finish_kernel(own_a, up_a, down_a, own_b, up_b, down_b, query, key, value, out):
    a = (own_a[...] + up_a[...].astype(F32) + down_a[...].astype(F32)).T
    b = (own_b[...] + up_b[...].astype(F32) + down_b[...].astype(F32)).T
    value[...] = a[:, :KW].astype(BF)
    out[...] = a[:, KW:].astype(BF)
    query[...] = b[:, :QW].astype(BF)
    key[...] = b[:, QW:].astype(BF)


def finish(own_a, near_a, own_b, near_b):
    shape = lambda n: jax.ShapeDtypeStruct((HEAD, n), BF)
    return pl.pallas_call(
        finish_kernel,
        in_specs=[vmem_spec()] * 6,
        out_specs=[vmem_spec()] * 4,
        out_shape=[shape(QW), shape(KW), shape(KW), shape(QW)],
        compiler_params=params(16),
        cost_estimate=cost(1e6, 2e6),
        name="finish",
    )(own_a, *near_a, own_b, *near_b)


def shift(value, axis, by):
    n = lax.axis_size(axis)
    return lax.ppermute(value, axis, [(i, (i + by) % n) for i in range(n)])


def both_ways(up, down, axis):
    return shift(up, axis, 1), shift(down, axis, -1)


def on_device(x, wq, wk, wv, wo, c, piece_doc, piece_offset, doc_owner):
    ix, iz, ic, iy = (lax.axis_index(a) for a in ("x", "z", "c", "tp"))
    me = (ix * NZ + iz) * NC + ic
    cos_table, sin_table = rotary_tables()
    sent = project(
        me.reshape(1), piece_doc, piece_offset, doc_owner, x, c, wq, wk, wv, wo, cos_table, sin_table
    )
    got = lax.all_to_all(sent, CTX, split_axis=0, concat_axis=0, tiled=True)
    where = jnp.stack([ix, iz, ic, iy]).astype(I32)
    xk, xs, ck, cs = regroup(where, sent, x, c)
    xr = shift(xs, "c", 1)
    cr = shift(cs, "c", 1)

    doc_grid = piece_doc.reshape(N_CTX, PIECES)
    own_doc = lax.dynamic_slice_in_dim(piece_doc, me * PIECES, PIECES)
    doc_ids = jnp.arange(doc_owner.shape[0], dtype=I32)
    own_owner = jnp.sum(jnp.where(own_doc[:, None] == doc_ids[None, :], doc_owner[None, :], 0), axis=1)
    ids = jnp.arange(PIECES, dtype=I32)
    order_key = own_owner * PIECES + ids
    slot = jnp.sum((order_key[None, :] < order_key[:, None]).astype(I32), axis=1)
    blocks = jnp.arange(TARGETS, dtype=I32) * (PAIR // PIECE)
    targets = jnp.sum(jnp.where(blocks[:, None] == slot[None, :], own_owner[None, :], 0), axis=1)
    within = jnp.arange(PIECE, dtype=I32)
    packed_row = (slot[:, None] * PIECE + within[None, :]).reshape(1, TOK)

    mine_doc = doc_owner == me
    doc_rank = jnp.sum((mine_doc[None, :] & (doc_ids[None, :] < doc_ids[:, None])).astype(I32), axis=1)
    four = jnp.arange(4, dtype=I32)
    my_docs = jnp.sum(
        jnp.where(mine_doc[None, :] & (doc_rank[None, :] == four[:, None]), doc_ids[None, :], 0), axis=1
    )
    mine = jnp.any(doc_grid[None, :, :] == my_docs[:, None, None], axis=0)
    before = (ids[:, None] < ids[None, :]).astype(BF)
    rank_in = jnp.dot(mine.astype(BF), before, preferred_element_type=F32).astype(I32)
    is_live = jnp.any(mine, axis=1)
    sources = jnp.arange(N_CTX, dtype=I32)
    live_rank = jnp.sum((is_live[None, :] & (sources[None, :] < sources[:, None])).astype(I32), axis=1)
    kth = jnp.arange(TARGETS, dtype=I32)
    live = jnp.sum(
        jnp.where(is_live[None, :] & (live_rank[None, :] == kth[:, None]), sources[None, :], 0), axis=1
    )
    index = jnp.where(mine, live_rank[:, None] * (PAIR // PIECE) + rank_in, -1).reshape(1, -1)
    chosen = index == ids[:, None]
    live_doc = jnp.sum(jnp.where(chosen, piece_doc[None, :], 0), axis=1)
    live_offset = jnp.sum(jnp.where(chosen, piece_offset[None, :], 0), axis=1)
    row_doc = jnp.repeat(live_doc, PIECE)
    row_pos = (live_offset[:, None] + within[None, :]).reshape(-1)

    back = attend(
        live,
        live_offset,
        got,
        cos_table,
        sin_table,
        row_doc[:, None],
        row_doc[None, :],
        row_pos[:, None],
        row_pos[None, :],
    )
    home = lax.all_to_all(back, CTX, split_axis=0, concat_axis=0, tiled=True)
    dy, y0, y1 = restore(where, targets, home, packed_row, wq, wk, wv)
    peer = shift(dy, "c", 1)
    y_far = both_ways(y0, y1, "tp")
    a0, a1, b0, b1 = weight_grad(dy, FAR, 1, True, dy, peer, xk, xr, ck, cr)
    a_far = both_ways(a0, a1, "x")
    b_far = both_ways(b0, b1, "z")
    y_near = input_grad(where, a0, UP, 2, dy, wq, wk, wv)
    a_near, b_near = weight_grad(y_near, UP, 2, False, dy, peer, xk, xr, ck, cr)
    y_sums = add_near((y_near, *y_far))
    y_got = both_ways(*y_sums, "tp")
    sums = add_near((a_near, *a_far), (b_near, *b_far))
    a_got = both_ways(*sums[:2], "x")
    b_got = both_ways(*sums[2:], "z")
    a_own, b_own = weight_grad(sums[0], OWN, 1, False, dy, peer, xk, xr, ck, cr)
    y_own = input_grad(where, a_own, OWN, 1, dy, wq, wk, wv)
    far = add_total(a_own, a_got, b_own, b_got)
    a_far = both_ways(far[0], far[1], "z")
    b_far = both_ways(far[4], far[5], "x")
    sums = add_near((far[2], *a_far), (far[6], *b_far))
    a_got = both_ways(*sums[:2], "z")
    b_got = both_ways(*sums[2:], "x")
    grad_in = (
        y_own.astype(F32) + y_got[0].astype(F32) + y_got[1].astype(F32)
    ).astype(BF)
    grad_query, grad_key, grad_value, grad_out = finish(far[3], a_got, far[7], b_got)
    return grad_in, grad_query, grad_key, grad_value, grad_out


def solution(mesh):
    fine = Mesh(mesh.devices.reshape(NX, NZ, NC, NT), ("x", "z", "c", "tp"))
    column = P(None, "tp")
    both = P(CTX, "tp")
    return jax.shard_map(
        on_device,
        mesh=fine,
        in_specs=(P(CTX, None), column, column, column, column, P(CTX, None), P(), P(), P()),
        out_specs=(both,) * 5,
        check_vma=False,
    )
```

```python
import functools
import math

import jax
import jax.numpy as jnp
import numpy as np
from jax import lax
from jax.experimental import pallas as pl
from jax.experimental.pallas import tpu as pltpu
from jax.sharding import Mesh, PartitionSpec as P


HEAD = 128
PIECE = 8
ROPE_BASE = 500000.0
FILL = -1e30
NX, NZ, NC, NT = 4, 4, 2, 4
CTX = ("x", "z", "c")
N_CTX = NX * NZ * NC
TOK = 512
WIDTH = 4096
QW = 512
KW = 128
COLS = 1280
K0, V0, G0 = 512, 640, 768
PAIR = 32
TARGETS = 16
PIECES = TOK // PIECE
MAX_POS = 512
HALF = 640
CUT = HALF // 2
FAR, UP, OWN, DOWN = 0, 1, 2, 3
SCALE = 1.0 / math.sqrt(HEAD)
BF = jnp.bfloat16
F32 = jnp.float32
I32 = jnp.int32
NN = (((1,), (0,)), ((), ()))
NTD = (((1,), (1,)), ((), ()))
TN = (((0,), (0,)), ((), ()))
TOKEN = jax.ShapeDtypeStruct((8, HEAD), F32)
TOKEN_SPEC = pl.BlockSpec((8, HEAD), lambda *_: (0, 0))


def dot(a, b, dims=NN):
    return lax.dot_general(a, b, dims, preferred_element_type=F32)


def vmem_spec():
    return pl.BlockSpec(memory_space=pltpu.VMEM)


def smem_spec():
    return pl.BlockSpec(memory_space=pltpu.SMEM)


def any_spec():
    return pl.BlockSpec(memory_space=pl.ANY)


def params(mib):
    return pltpu.CompilerParams(vmem_limit_bytes=mib * 1024 * 1024)


def cost(flops, nbytes):
    return pl.CostEstimate(flops=int(flops), bytes_accessed=int(nbytes), transcendentals=0)


def rotary_tables():
    half = HEAD // 2
    frequency = np.float32(ROPE_BASE) ** (-2.0 * np.arange(half, dtype=np.float32) / np.float32(HEAD))
    angles = np.arange(MAX_POS, dtype=np.float32)[:, None] * frequency.astype(np.float32)[None, :]
    cosine, sine = np.cos(angles), np.sin(angles)
    return (
        jnp.asarray(np.concatenate([cosine, cosine], axis=1).astype(np.float32)),
        jnp.asarray(np.concatenate([-sine, sine], axis=1).astype(np.float32)),
    )


def related(coordinate, order):
    return (coordinate + 2 - order) & 3


def store_blocks(rows, target, which, sems):
    copies = [
        pltpu.make_async_copy(rows.at[pl.ds(k * PAIR, PAIR)], target.at[which[k]], sems.at[k])
        for k in range(TARGETS)
    ]
    for copy in copies:
        copy.start()
    return copies


def project_kernel(
    me,
    piece_doc,
    piece_offset,
    doc_owner,
    x_hbm,
    c_hbm,
    wq_hbm,
    wk_hbm,
    wv_hbm,
    wo_hbm,
    cos_table,
    sin_table,
    out_ref,
    token,
    x_ref,
    c_ref,
    wq_ref,
    wkv_ref,
    wo_ref,
    made,
    packed,
    final,
    slot_of,
    count,
    first,
    targets,
    load_sems,
    sems,
):
    span = 2 * HEAD
    copy = pltpu.make_async_copy
    token[...] = jnp.zeros_like(token)
    get_x = copy(x_hbm, x_ref, load_sems.at[0])
    get_k = copy(wk_hbm, wkv_ref.at[:, pl.ds(0, KW)], load_sems.at[1])
    get_v = copy(wv_hbm, wkv_ref.at[:, pl.ds(KW, KW)], load_sems.at[2])
    get_c = copy(c_hbm, c_ref, load_sems.at[3])

    def part(i, source, into, sem):
        at = pl.ds(pl.multiple_of(i * span, span), span)
        return copy(source.at[:, at], into.at[i], load_sems.at[sem + i])

    get_x.start()
    get_k.start()
    get_v.start()
    for i in range(2):
        part(i, wq_hbm, wq_ref, 4).start()
    get_c.start()
    for i in range(2):
        part(i, wo_hbm, wo_ref, 6).start()

    for o in range(N_CTX):
        count[o] = 0
    for i in range(PIECES):
        owner = doc_owner[piece_doc[me[0] * PIECES + i]]
        slot_of[i] = owner * PIECES + count[owner]
        count[owner] = count[owner] + 1
    run = jnp.int32(0)
    for o in range(N_CTX):
        first[o] = run
        targets[run >> 2] = jnp.int32(o)
        run = run + count[o]
    for i in range(PIECES):
        key = slot_of[i]
        slot_of[i] = (first[key >> 6] + (key & (PIECES - 1))) * PIECE

    def pack(base, rotated):
        for i in range(PIECES):
            to = pl.multiple_of(slot_of[i], PIECE)
            here = slice(i * PIECE, (i + 1) * PIECE)
            if rotated:
                at = pl.multiple_of(piece_offset[me[0] * PIECES + i], PIECE)
                cosine = cos_table[pl.ds(at, PIECE), :]
                sine = sin_table[pl.ds(at, PIECE), :]
            for h in range(2):
                u = made[here, h * HEAD : (h + 1) * HEAD]
                if h < rotated:
                    u = u * cosine + pltpu.roll(u, HEAD // 2, 1) * sine
                packed[pl.ds(to, PIECE), h * HEAD : (h + 1) * HEAD] = u
        final[:, pl.ds(base, span)] = packed[...].astype(BF)

    get_x.wait()
    get_k.wait()
    get_v.wait()
    made[...] = dot(x_ref[...], wkv_ref[...])
    pack(K0, 1)

    @pl.loop(0, 2)
    def _(i):
        part(i, wq_hbm, wq_ref, 4).wait()
        made[...] = dot(x_ref[...], wq_ref[i])
        pack(pl.multiple_of(i * span, span), 2)

    get_c.wait()

    @pl.loop(0, 2)
    def _(i):
        part(i, wo_hbm, wo_ref, 6).wait()
        made[...] = dot(c_ref[...], wo_ref[i])
        pack(pl.multiple_of(G0 + i * span, span), 0)

    for each in store_blocks(final, out_ref, targets, sems):
        each.wait()


def project(me, piece_doc, piece_offset, doc_owner, x, c, wq, wk, wv, wo, cos_table, sin_table):
    span = 2 * HEAD
    smem = pltpu.SMEM
    return pl.pallas_call(
        project_kernel,
        in_specs=[smem_spec()] * 4 + [any_spec()] * 6 + [vmem_spec()] * 2,
        out_specs=[any_spec(), vmem_spec()],
        scratch_shapes=[
            pltpu.VMEM((TOK, WIDTH), BF),
            pltpu.VMEM((TOK, WIDTH), BF),
            pltpu.VMEM((2, WIDTH, span), BF),
            pltpu.VMEM((WIDTH, 2 * KW), BF),
            pltpu.VMEM((2, WIDTH, span), BF),
            pltpu.VMEM((TOK, span), F32),
            pltpu.VMEM((TOK, span), F32),
            pltpu.VMEM((TOK, COLS), BF),
            smem((PIECES,), I32),
            smem((N_CTX,), I32),
            smem((N_CTX,), I32),
            smem((N_CTX,), I32),
            pltpu.SemaphoreType.DMA((8,)),
            pltpu.SemaphoreType.DMA((TARGETS,)),
        ],
        out_shape=[jax.ShapeDtypeStruct((N_CTX, PAIR, COLS), BF), TOKEN],
        compiler_params=params(60),
        cost_estimate=cost(6e9, 24e6),
        name="project",
    )(me, piece_doc, piece_offset, doc_owner, x, c, wq, wk, wv, wo, cos_table, sin_table)


def regroup_kernel(where, after, x_ref, c_ref, xk_ref, xs_ref, ck_ref, cs_ref, token):
    token[...] = jnp.zeros_like(token)
    core = where[2]
    for i in range(NZ):
        base = related(where[1], i) * 2
        keep = pl.ds(pl.multiple_of((base + core) * HEAD, HEAD), HEAD)
        send = pl.ds(pl.multiple_of((base + 1 - core) * HEAD, HEAD), HEAD)
        xk_ref[i] = x_ref[:, keep]
        xs_ref[i] = x_ref[:, send]
        ck_ref[i] = c_ref[:, keep]
        cs_ref[i] = c_ref[:, send]


def regroup(where, after, x, c):
    part = pl.BlockSpec((TOK, WIDTH // NX), lambda i, where: (0, related(where[0], i)))
    half = jax.ShapeDtypeStruct((NX * NZ, TOK, HEAD), BF)
    return pl.pallas_call(
        regroup_kernel,
        grid_spec=pltpu.PrefetchScalarGridSpec(
            num_scalar_prefetch=1,
            grid=(NX,),
            in_specs=[any_spec(), part, part],
            out_specs=[pl.BlockSpec((NZ, TOK, HEAD), lambda i, where: (i, 0, 0))] * 4 + [TOKEN_SPEC],
        ),
        out_shape=[half] * 4 + [TOKEN],
        compiler_params=params(16),
        cost_estimate=cost(1, 17e6),
        name="regroup",
    )(where, after, x, c)


def fetch_blocks(source, which, rows, sems):
    copies = [
        pltpu.make_async_copy(source.at[which[k]], rows.at[pl.ds(k * PAIR, PAIR)], sems.at[k])
        for k in range(TARGETS)
    ]
    for copy in copies:
        copy.start()
    return copies


def attend_kernel(
    live,
    offsets,
    got_ref,
    cos_table,
    sin_table,
    doc_col,
    doc_row,
    pos_col,
    pos_row,
    token_x,
    token_f,
    token_r,
    out_ref,
    rows,
    back,
    bias,
    cos_rows,
    sin_rows,
    sems,
):
    copies = fetch_blocks(got_ref, live, rows, sems)
    for i in range(PIECES):
        at = pl.multiple_of(offsets[i], PIECE)
        cos_rows[i * PIECE : (i + 1) * PIECE, :] = cos_table[pl.ds(at, PIECE), :]
        sin_rows[i * PIECE : (i + 1) * PIECE, :] = sin_table[pl.ds(at, PIECE), :]
    allowed = (doc_col[...] == doc_row[...]) & (pos_row[...] <= pos_col[...])
    bias[...] = jnp.where(allowed, 0.0, FILL)
    for copy in copies:
        copy.wait()
    keys = rows[:, K0:V0]
    values = rows[:, V0:G0]
    key_grad = jnp.zeros((TOK, HEAD), F32)
    value_grad = jnp.zeros((TOK, HEAD), F32)
    half = HEAD // 2

    def unrotate(u):
        return u * cos_rows[...] - pltpu.roll(u, half, 1) * sin_rows[...]

    for h in range(QW // HEAD):
        here = slice(h * HEAD, (h + 1) * HEAD)
        there = slice(G0 + h * HEAD, G0 + (h + 1) * HEAD)
        query = rows[:, here]
        grads = rows[:, there]
        scores = dot(query, keys, NTD) * SCALE + bias[...]
        weight = jnp.exp(scores - jnp.max(scores, axis=1, keepdims=True))
        prob = weight * (1.0 / jnp.sum(weight, axis=1, keepdims=True))
        rounded = prob.astype(BF)
        attended = dot(rounded, values).astype(BF)
        back[:, there] = attended
        delta = jnp.sum(grads.astype(F32) * attended.astype(F32), axis=1, keepdims=True)
        prob_grad = dot(grads, values, NTD)
        score_grad = (prob * (prob_grad - delta)).astype(BF)
        back[:, here] = unrotate(dot(score_grad, keys) * SCALE).astype(BF)
        key_grad = key_grad + dot(score_grad, query, TN)
        value_grad = value_grad + dot(rounded, grads, TN)
    back[:, K0:V0] = unrotate(key_grad * SCALE).astype(BF)
    back[:, V0:G0] = value_grad.astype(BF)
    for k in range(TARGETS):
        out_ref[live[k]] = back[k * PAIR : (k + 1) * PAIR, :]


def attend(live, offsets, got, cos_table, sin_table, doc_col, doc_row, pos_col, pos_row, *tokens):
    return pl.pallas_call(
        attend_kernel,
        in_specs=[smem_spec(), smem_spec(), any_spec()] + [vmem_spec()] * 6 + [any_spec()] * 3,
        out_specs=vmem_spec(),
        out_shape=jax.ShapeDtypeStruct((N_CTX, PAIR, COLS), BF),
        scratch_shapes=[
            pltpu.VMEM((TOK, COLS), BF),
            pltpu.VMEM((TOK, COLS), BF),
            pltpu.VMEM((TOK, TOK), F32),
            pltpu.VMEM((TOK, HEAD), F32),
            pltpu.VMEM((TOK, HEAD), F32),
            pltpu.SemaphoreType.DMA((TARGETS,)),
        ],
        compiler_params=params(28),
        cost_estimate=cost(4e9, 6e6),
        name="attend",
    )(live, offsets, got, cos_table, sin_table, doc_col, doc_row, pos_col, pos_row, *tokens)


def stage_kernel(where, after, wq_ref, wk_ref, wv_ref, out_ref, token):
    token[...] = jnp.zeros_like(token)
    out_ref[:, :K0] = wq_ref[...]
    out_ref[:, K0:V0] = wk_ref[...]
    out_ref[:, V0:] = wv_ref[...]


def stage_weights(where, after, at, count, wq, wk, wv):
    span = WIDTH // NT
    block = lambda i, where: (related(where[3], at + i), 0)
    return pl.pallas_call(
        stage_kernel,
        grid_spec=pltpu.PrefetchScalarGridSpec(
            num_scalar_prefetch=1,
            grid=(count,),
            in_specs=[
                any_spec(),
                pl.BlockSpec((span, QW), block),
                pl.BlockSpec((span, KW), block),
                pl.BlockSpec((span, KW), block),
            ],
            out_specs=[pl.BlockSpec((span, G0), lambda i, *_: (i, 0)), TOKEN_SPEC],
        ),
        out_shape=[jax.ShapeDtypeStruct((count * span, G0), BF), TOKEN],
        compiler_params=params(12),
        cost_estimate=cost(1, 3e6 * count),
        name="stage_weights",
    )(where, after, wq, wk, wv)


def restore_kernel(targets, got_ref, rows_ref, out_ref, packed, sems):
    copies = fetch_blocks(got_ref, targets, packed, sems)
    slot = lax.broadcasted_iota(I32, (TOK, TOK), 0)
    one_hot = jnp.where(slot == rows_ref[...], 1.0, 0.0).astype(BF)
    for copy in copies:
        copy.wait()
    out_ref[...] = dot(one_hot, packed[...], TN).astype(BF)


def restore(targets, got, rows):
    return pl.pallas_call(
        restore_kernel,
        in_specs=[smem_spec(), any_spec(), vmem_spec()],
        out_specs=vmem_spec(),
        out_shape=jax.ShapeDtypeStruct((TOK, COLS), BF),
        scratch_shapes=[pltpu.VMEM((TOK, COLS), BF), pltpu.SemaphoreType.DMA((TARGETS,))],
        compiler_params=params(16),
        cost_estimate=cost(0.7e9, 4e6),
        name="restore",
    )(targets, got, rows)


def input_grad_kernel(after, dy_ref, w_ref, *outs):
    total = dot(dy_ref[:, :G0], w_ref[...], NTD).astype(BF)
    if len(outs) == 1:
        outs[0][...] = total
    else:
        outs[0][...] = total[: TOK // 2]
        outs[1][...] = total[TOK // 2 :]


def input_grad(after, at, count, dy, weights, split=False):
    span = WIDTH // NT
    if split:
        out_shape = [jax.ShapeDtypeStruct((TOK // 2, span), BF)] * 2
        out_specs = [pl.BlockSpec((TOK // 2, span), lambda i: (0, 0))] * 2
    else:
        out_shape = jax.ShapeDtypeStruct((count * TOK, span), BF)
        out_specs = pl.BlockSpec((TOK, span), lambda i: (i, 0))
    return pl.pallas_call(
        input_grad_kernel,
        grid=(count,),
        in_specs=[
            any_spec(),
            pl.BlockSpec((TOK, COLS), lambda i: (0, 0)),
            pl.BlockSpec((span, G0), lambda i: (at + 2 * i, 0)),
        ],
        out_specs=out_specs,
        out_shape=out_shape,
        compiler_params=params(20),
        cost_estimate=cost(0.8e9 * count, 5e6 * count),
        name="input_grad",
    )(after, dy, weights)


def weight_grad_kernel(after, own, peer, xa0, xa1, c0, c1, b00, b01, b02, b03, b10, b11, b12, b13, *outs):
    wide = lambda ref: jnp.concatenate([ref[j] for j in range(NZ)], axis=1)
    join = lambda refs: jnp.concatenate([ref[0] for ref in refs], axis=1)
    first = dot(own[:, V0:G0], wide(xa0), TN) + dot(peer[:, V0:G0], wide(xa1), TN)
    second = dot(own[:, G0:], wide(c0), TN) + dot(peer[:, G0:], wide(c1), TN)
    third = dot(own[:, :V0], join([b00, b01, b02, b03]), TN) + dot(
        peer[:, :V0], join([b10, b11, b12, b13]), TN
    )
    if len(outs) == 4:
        a0, a1, b0, b1 = outs
        a0[:KW, :] = first.astype(BF)
        a0[KW:, :] = second[: CUT - KW].astype(BF)
        a1[...] = second[CUT - KW :].astype(BF)
        b0[...] = third[:CUT].astype(BF)
        b1[...] = third[CUT:].astype(BF)
    else:
        a, b = outs
        a[:KW, :] = first.astype(BF)
        a[KW:, :] = second.astype(BF)
        b[...] = third.astype(BF)


def weight_grad(after, at, count, split, own, peer, xk, xr, ck, cr):
    wide = NZ * HEAD
    whole = lambda i: (0, 0)
    spec_a = pl.BlockSpec((NZ, TOK, HEAD), lambda i: (at + 2 * i, 0, 0))
    specs_b = [
        pl.BlockSpec((1, TOK, HEAD), functools.partial(lambda j, i: (j * NZ + at + 2 * i, 0, 0), j))
        for j in range(NX)
    ]
    if split:
        out_shape = [jax.ShapeDtypeStruct((CUT, wide), BF)] * 4
        out_specs = [pl.BlockSpec((CUT, wide), whole)] * 4
    else:
        out_shape = [jax.ShapeDtypeStruct((count * HALF, wide), BF)] * 2
        out_specs = [pl.BlockSpec((HALF, wide), lambda i: (i, 0))] * 2
    return pl.pallas_call(
        weight_grad_kernel,
        grid=(count,),
        in_specs=[any_spec(), pl.BlockSpec((TOK, COLS), whole), pl.BlockSpec((TOK, COLS), whole)]
        + [spec_a] * 4
        + specs_b
        + specs_b,
        out_specs=out_specs,
        out_shape=out_shape,
        compiler_params=params(28),
        cost_estimate=cost(1.4e9 * count, 6e6 * count),
        name="weight_grad",
    )(after, own, peer, xk, xr, ck, cr, xk, xk, xk, xk, xr, xr, xr, xr)


def near_kernel(count, *refs):
    for g in range(count):
        near, below, above = refs[3 * g : 3 * g + 3]
        up, down = refs[3 * count + 2 * g : 3 * count + 2 * g + 2]
        rows = up.shape[0]
        cut = rows // 2
        up[:cut] = (near[:cut].astype(F32) + below[...].astype(F32)).astype(BF)
        up[cut:] = near[cut:rows]
        down[:cut] = near[rows : rows + cut]
        down[cut:] = (near[rows + cut :].astype(F32) + above[...].astype(F32)).astype(BF)


def add_near(*groups):
    flat = [value for group in groups for value in group]
    shapes = []
    for near, _, _ in groups:
        shapes += [jax.ShapeDtypeStruct((near.shape[0] // 2, near.shape[1]), BF)] * 2
    return pl.pallas_call(
        functools.partial(near_kernel, len(groups)),
        in_specs=[vmem_spec()] * len(flat),
        out_specs=[vmem_spec()] * len(shapes),
        out_shape=shapes,
        compiler_params=params(16),
        cost_estimate=cost(1e6, 5e6),
        name="add_near",
    )(*flat)


def total_kernel(own_a, up_a, down_a, own_b, up_b, down_b, *outs):
    for g, (own, up, down) in enumerate(((own_a, up_a, down_a), (own_b, up_b, down_b))):
        total = own[...].astype(F32) + up[...].astype(F32) + down[...].astype(F32)
        for place in range(NZ):
            ref = outs[4 * g + place]
            ref[...] = total[:, place * HEAD : (place + 1) * HEAD].astype(ref.dtype)


def add_total(own_a, near_a, own_b, near_b):
    one = [jax.ShapeDtypeStruct((HALF, HEAD), F32 if place == OWN else BF) for place in range(NZ)]
    return pl.pallas_call(
        total_kernel,
        in_specs=[vmem_spec()] * 6,
        out_specs=[vmem_spec()] * 8,
        out_shape=one + one,
        compiler_params=params(16),
        cost_estimate=cost(1e6, 5e6),
        name="add_total",
    )(own_a, *near_a, own_b, *near_b)


def finish_kernel(*refs):
    ins, (query, key, value, out) = refs[:8], refs[8:]
    a, b = (sum(ref[...].astype(F32) for ref in ins[4 * g : 4 * g + 4]).T for g in range(2))
    value[...] = a[:, :KW].astype(BF)
    out[...] = a[:, KW:].astype(BF)
    query[...] = b[:, :QW].astype(BF)
    key[...] = b[:, QW:].astype(BF)


def finish(own_a, got_a, own_b, got_b):
    shape = lambda n: jax.ShapeDtypeStruct((HEAD, n), BF)
    return pl.pallas_call(
        finish_kernel,
        in_specs=[vmem_spec()] * 8,
        out_specs=[vmem_spec()] * 4,
        out_shape=[shape(QW), shape(KW), shape(KW), shape(QW)],
        compiler_params=params(16),
        cost_estimate=cost(1e6, 2e6),
        name="finish",
    )(own_a, *got_a, own_b, *got_b)


def shift(value, axis, by):
    n = lax.axis_size(axis)
    return lax.ppermute(value, axis, [(i, (i + by) % n) for i in range(n)])


def both_ways(up, down, axis):
    return shift(up, axis, 1), shift(down, axis, -1)


def all_ways(parts, axis):
    return shift(parts[FAR], axis, 2), shift(parts[UP], axis, 1), shift(parts[DOWN], axis, -1)


def on_device(x, wq, wk, wv, wo, c, piece_doc, piece_offset, doc_owner):
    ix, iz, ic, iy = (lax.axis_index(a) for a in ("x", "z", "c", "tp"))
    me = (ix * NZ + iz) * NC + ic
    cos_table, sin_table = rotary_tables()
    sent, token_p = project(
        me.reshape(1), piece_doc, piece_offset, doc_owner, x, c, wq, wk, wv, wo, cos_table, sin_table
    )
    got = lax.all_to_all(sent, CTX, split_axis=0, concat_axis=0, tiled=True)
    where = jnp.stack([ix, iz, ic, iy]).astype(I32)
    xk, xs, ck, cs, token_x = regroup(where, token_p, x, c)
    w_far, token_f = stage_weights(where, token_p, FAR, 1, wq, wk, wv)
    w_rest, token_r = stage_weights(where, token_p, UP, 3, wq, wk, wv)
    xr = shift(xs, "c", 1)
    cr = shift(cs, "c", 1)

    doc_grid = piece_doc.reshape(N_CTX, PIECES)
    own_doc = lax.dynamic_slice_in_dim(piece_doc, me * PIECES, PIECES)
    doc_ids = jnp.arange(doc_owner.shape[0], dtype=I32)
    own_owner = jnp.sum(jnp.where(own_doc[:, None] == doc_ids[None, :], doc_owner[None, :], 0), axis=1)
    ids = jnp.arange(PIECES, dtype=I32)
    order_key = own_owner * PIECES + ids
    slot = jnp.sum((order_key[None, :] < order_key[:, None]).astype(I32), axis=1)
    blocks = jnp.arange(TARGETS, dtype=I32) * (PAIR // PIECE)
    targets = jnp.sum(jnp.where(blocks[:, None] == slot[None, :], own_owner[None, :], 0), axis=1)
    within = jnp.arange(PIECE, dtype=I32)
    packed_row = (slot[:, None] * PIECE + within[None, :]).reshape(1, TOK)

    mine_doc = doc_owner == me
    doc_rank = jnp.sum((mine_doc[None, :] & (doc_ids[None, :] < doc_ids[:, None])).astype(I32), axis=1)
    four = jnp.arange(4, dtype=I32)
    my_docs = jnp.sum(
        jnp.where(mine_doc[None, :] & (doc_rank[None, :] == four[:, None]), doc_ids[None, :], 0), axis=1
    )
    mine = jnp.any(doc_grid[None, :, :] == my_docs[:, None, None], axis=0)
    before = (ids[:, None] < ids[None, :]).astype(BF)
    rank_in = jnp.dot(mine.astype(BF), before, preferred_element_type=F32).astype(I32)
    is_live = jnp.any(mine, axis=1)
    sources = jnp.arange(N_CTX, dtype=I32)
    live_rank = jnp.sum((is_live[None, :] & (sources[None, :] < sources[:, None])).astype(I32), axis=1)
    kth = jnp.arange(TARGETS, dtype=I32)
    live = jnp.sum(
        jnp.where(is_live[None, :] & (live_rank[None, :] == kth[:, None]), sources[None, :], 0), axis=1
    )
    index = jnp.where(mine, live_rank[:, None] * (PAIR // PIECE) + rank_in, -1).reshape(1, -1)
    chosen = index == ids[:, None]
    live_doc = jnp.sum(jnp.where(chosen, piece_doc[None, :], 0), axis=1)
    live_offset = jnp.sum(jnp.where(chosen, piece_offset[None, :], 0), axis=1)
    row_doc = jnp.repeat(live_doc, PIECE)
    row_pos = (live_offset[:, None] + within[None, :]).reshape(-1)

    back = attend(
        live,
        live_offset,
        got,
        cos_table,
        sin_table,
        row_doc[:, None],
        row_doc[None, :],
        row_pos[:, None],
        row_pos[None, :],
        token_x,
        token_f,
        token_r,
    )
    home = lax.all_to_all(back, CTX, split_axis=0, concat_axis=0, tiled=True)
    dy = restore(targets, home, packed_row)
    peer = shift(dy, "c", 1)
    y0, y1 = input_grad(dy, 0, 1, dy, w_far, split=True)
    a0, a1, b0, b1 = weight_grad(y0, FAR, 1, True, dy, peer, xk, xr, ck, cr)
    y0, y1, a0, a1, b0, b1 = lax.optimization_barrier((y0, y1, a0, a1, b0, b1))
    a_far = both_ways(a0, a1, "x")
    b_far = both_ways(b0, b1, "z")
    y_far = both_ways(y0, y1, "tp")
    a_near, b_near = weight_grad(a0, UP, 2, False, dy, peer, xk, xr, ck, cr)
    sums = add_near((a_near, *a_far), (b_near, *b_far))
    a_got = both_ways(*sums[:2], "x")
    b_got = both_ways(*sums[2:], "z")
    y_near = input_grad(sums[0], UP - 1, 2, dy, w_rest)
    y_sums = add_near((y_near, *y_far))
    y_got = both_ways(*y_sums, "tp")
    a_own, b_own = weight_grad(y_near, OWN, 1, False, dy, peer, xk, xr, ck, cr)
    y_own = input_grad(a_own, OWN - 1, 1, dy, w_rest)
    parts = add_total(a_own, a_got, b_own, b_got)
    a_got = all_ways(parts[:4], "z")
    b_got = all_ways(parts[4:], "x")
    grad_in = (
        y_own.astype(F32) + y_got[0].astype(F32) + y_got[1].astype(F32)
    ).astype(BF)
    grad_query, grad_key, grad_value, grad_out = finish(parts[OWN], a_got, parts[4 + OWN], b_got)
    return grad_in, grad_query, grad_key, grad_value, grad_out


def solution(mesh):
    fine = Mesh(mesh.devices.reshape(NX, NZ, NC, NT), ("x", "z", "c", "tp"))
    column = P(None, "tp")
    both = P(CTX, "tp")
    return jax.shard_map(
        on_device,
        mesh=fine,
        in_specs=(P(CTX, None), column, column, column, column, P(CTX, None), P(), P(), P()),
        out_specs=(both,) * 5,
        check_vma=False,
    )
```

```python
import functools
import math

import jax
import jax.numpy as jnp
import numpy as np
from jax import lax
from jax.experimental import pallas as pl
from jax.experimental.pallas import tpu as pltpu
from jax.sharding import Mesh, PartitionSpec as P


HEAD = 128
PIECE = 8
ROPE_BASE = 500000.0
FILL = -1e30
NX, NZ, NC, NT = 4, 4, 2, 4
CTX = ("x", "z", "c")
N_CTX = NX * NZ * NC
TOK = 512
WIDTH = 4096
QW = 512
KW = 128
COLS = 1280
K0, V0, G0 = 512, 640, 768
PAIR = 32
TARGETS = 16
PIECES = TOK // PIECE
MAX_POS = 512
HALF = 640
CUT = HALF // 2
FAR, UP, OWN, DOWN = 0, 1, 2, 3
SCALE = 1.0 / math.sqrt(HEAD)
BF = jnp.bfloat16
F32 = jnp.float32
I32 = jnp.int32
NN = (((1,), (0,)), ((), ()))
NTD = (((1,), (1,)), ((), ()))
TN = (((0,), (0,)), ((), ()))
TOKEN = jax.ShapeDtypeStruct((8, HEAD), F32)
TOKEN_SPEC = pl.BlockSpec((8, HEAD), lambda *_: (0, 0))


def dot(a, b, dims=NN):
    return lax.dot_general(a, b, dims, preferred_element_type=F32)


def vmem_spec():
    return pl.BlockSpec(memory_space=pltpu.VMEM)


def smem_spec():
    return pl.BlockSpec(memory_space=pltpu.SMEM)


def any_spec():
    return pl.BlockSpec(memory_space=pl.ANY)


def params(mib):
    return pltpu.CompilerParams(vmem_limit_bytes=mib * 1024 * 1024)


def cost(flops, nbytes):
    return pl.CostEstimate(flops=int(flops), bytes_accessed=int(nbytes), transcendentals=0)


def rotary_tables():
    half = HEAD // 2
    frequency = np.float32(ROPE_BASE) ** (-2.0 * np.arange(half, dtype=np.float32) / np.float32(HEAD))
    angles = np.arange(MAX_POS, dtype=np.float32)[:, None] * frequency.astype(np.float32)[None, :]
    cosine, sine = np.cos(angles), np.sin(angles)
    return (
        jnp.asarray(np.concatenate([cosine, cosine], axis=1).astype(np.float32)),
        jnp.asarray(np.concatenate([-sine, sine], axis=1).astype(np.float32)),
    )


def related(coordinate, order):
    return (coordinate + 2 - order) & 3


def store_blocks(rows, target, which, sems):
    copies = [
        pltpu.make_async_copy(rows.at[pl.ds(k * PAIR, PAIR)], target.at[which[k]], sems.at[k])
        for k in range(TARGETS)
    ]
    for copy in copies:
        copy.start()
    return copies


def project_kernel(
    me,
    piece_doc,
    piece_offset,
    doc_owner,
    x_hbm,
    c_hbm,
    wq_hbm,
    wk_hbm,
    wv_hbm,
    wo_hbm,
    cos_table,
    sin_table,
    out_ref,
    token,
    x_ref,
    c_ref,
    wq_ref,
    wkv_ref,
    wo_ref,
    made,
    packed,
    final,
    slot_of,
    count,
    first,
    targets,
    load_sems,
    sems,
):
    span = 2 * HEAD
    copy = pltpu.make_async_copy
    token[...] = jnp.zeros_like(token)
    get_x = copy(x_hbm, x_ref, load_sems.at[0])
    get_k = copy(wk_hbm, wkv_ref.at[:, pl.ds(0, KW)], load_sems.at[1])
    get_v = copy(wv_hbm, wkv_ref.at[:, pl.ds(KW, KW)], load_sems.at[2])
    get_c = copy(c_hbm, c_ref, load_sems.at[3])

    def part(i, source, into, sem):
        at = pl.ds(pl.multiple_of(i * span, span), span)
        return copy(source.at[:, at], into.at[i], load_sems.at[sem + i])

    get_x.start()
    get_k.start()
    get_v.start()
    for i in range(2):
        part(i, wq_hbm, wq_ref, 4).start()
    get_c.start()
    for i in range(2):
        part(i, wo_hbm, wo_ref, 6).start()

    for o in range(N_CTX):
        count[o] = 0
    for i in range(PIECES):
        owner = doc_owner[piece_doc[me[0] * PIECES + i]]
        slot_of[i] = owner * PIECES + count[owner]
        count[owner] = count[owner] + 1
    run = jnp.int32(0)
    for o in range(N_CTX):
        first[o] = run
        targets[run >> 2] = jnp.int32(o)
        run = run + count[o]
    for i in range(PIECES):
        key = slot_of[i]
        slot_of[i] = (first[key >> 6] + (key & (PIECES - 1))) * PIECE

    def pack(base, rotated):
        for i in range(PIECES):
            to = pl.multiple_of(slot_of[i], PIECE)
            here = slice(i * PIECE, (i + 1) * PIECE)
            if rotated:
                at = pl.multiple_of(piece_offset[me[0] * PIECES + i], PIECE)
                cosine = cos_table[pl.ds(at, PIECE), :]
                sine = sin_table[pl.ds(at, PIECE), :]
            for h in range(2):
                u = made[here, h * HEAD : (h + 1) * HEAD]
                if h < rotated:
                    u = u * cosine + pltpu.roll(u, HEAD // 2, 1) * sine
                packed[pl.ds(to, PIECE), h * HEAD : (h + 1) * HEAD] = u
        final[:, pl.ds(base, span)] = packed[...].astype(BF)

    get_x.wait()
    get_k.wait()
    get_v.wait()
    made[...] = dot(x_ref[...], wkv_ref[...])
    pack(K0, 1)

    @pl.loop(0, 2)
    def _(i):
        part(i, wq_hbm, wq_ref, 4).wait()
        made[...] = dot(x_ref[...], wq_ref[i])
        pack(pl.multiple_of(i * span, span), 2)

    get_c.wait()

    @pl.loop(0, 2)
    def _(i):
        part(i, wo_hbm, wo_ref, 6).wait()
        made[...] = dot(c_ref[...], wo_ref[i])
        pack(pl.multiple_of(G0 + i * span, span), 0)

    for each in store_blocks(final, out_ref, targets, sems):
        each.wait()


def project(me, piece_doc, piece_offset, doc_owner, x, c, wq, wk, wv, wo, cos_table, sin_table):
    span = 2 * HEAD
    smem = pltpu.SMEM
    return pl.pallas_call(
        project_kernel,
        in_specs=[smem_spec()] * 4 + [any_spec()] * 6 + [vmem_spec()] * 2,
        out_specs=[any_spec(), vmem_spec()],
        scratch_shapes=[
            pltpu.VMEM((TOK, WIDTH), BF),
            pltpu.VMEM((TOK, WIDTH), BF),
            pltpu.VMEM((2, WIDTH, span), BF),
            pltpu.VMEM((WIDTH, 2 * KW), BF),
            pltpu.VMEM((2, WIDTH, span), BF),
            pltpu.VMEM((TOK, span), F32),
            pltpu.VMEM((TOK, span), F32),
            pltpu.VMEM((TOK, COLS), BF),
            smem((PIECES,), I32),
            smem((N_CTX,), I32),
            smem((N_CTX,), I32),
            smem((N_CTX,), I32),
            pltpu.SemaphoreType.DMA((8,)),
            pltpu.SemaphoreType.DMA((TARGETS,)),
        ],
        out_shape=[jax.ShapeDtypeStruct((N_CTX, PAIR, COLS), BF), TOKEN],
        compiler_params=params(60),
        cost_estimate=cost(6e9, 24e6),
        name="project",
    )(me, piece_doc, piece_offset, doc_owner, x, c, wq, wk, wv, wo, cos_table, sin_table)


def regroup_kernel(where, after, x_ref, c_ref, xk_ref, xs_ref, ck_ref, cs_ref, token):
    token[...] = jnp.zeros_like(token)
    core = where[2]
    for i in range(NZ):
        base = related(where[1], i) * 2
        keep = pl.ds(pl.multiple_of((base + core) * HEAD, HEAD), HEAD)
        send = pl.ds(pl.multiple_of((base + 1 - core) * HEAD, HEAD), HEAD)
        xk_ref[i] = x_ref[:, keep]
        xs_ref[i] = x_ref[:, send]
        ck_ref[i] = c_ref[:, keep]
        cs_ref[i] = c_ref[:, send]


def regroup(where, after, x, c):
    part = pl.BlockSpec((TOK, WIDTH // NX), lambda i, where: (0, related(where[0], i)))
    half = jax.ShapeDtypeStruct((NX * NZ, TOK, HEAD), BF)
    return pl.pallas_call(
        regroup_kernel,
        grid_spec=pltpu.PrefetchScalarGridSpec(
            num_scalar_prefetch=1,
            grid=(NX,),
            in_specs=[any_spec(), part, part],
            out_specs=[pl.BlockSpec((NZ, TOK, HEAD), lambda i, where: (i, 0, 0))] * 4 + [TOKEN_SPEC],
        ),
        out_shape=[half] * 4 + [TOKEN],
        compiler_params=params(16),
        cost_estimate=cost(1, 17e6),
        name="regroup",
    )(where, after, x, c)


def fetch_blocks(source, which, rows, sems):
    copies = [
        pltpu.make_async_copy(source.at[which[k]], rows.at[pl.ds(k * PAIR, PAIR)], sems.at[k])
        for k in range(TARGETS)
    ]
    for copy in copies:
        copy.start()
    return copies


def attend_kernel(
    live,
    offsets,
    got_ref,
    cos_table,
    sin_table,
    doc_col,
    doc_row,
    pos_col,
    pos_row,
    token_x,
    token_f,
    token_r,
    out_ref,
    rows,
    back,
    bias,
    cos_rows,
    sin_rows,
    sems,
):
    copies = fetch_blocks(got_ref, live, rows, sems)
    for i in range(PIECES):
        at = pl.multiple_of(offsets[i], PIECE)
        cos_rows[i * PIECE : (i + 1) * PIECE, :] = cos_table[pl.ds(at, PIECE), :]
        sin_rows[i * PIECE : (i + 1) * PIECE, :] = sin_table[pl.ds(at, PIECE), :]
    allowed = (doc_col[...] == doc_row[...]) & (pos_row[...] <= pos_col[...])
    bias[...] = jnp.where(allowed, 0.0, FILL)
    for copy in copies:
        copy.wait()
    keys = rows[:, K0:V0]
    values = rows[:, V0:G0]
    key_grad = jnp.zeros((TOK, HEAD), F32)
    value_grad = jnp.zeros((TOK, HEAD), F32)
    half = HEAD // 2

    def unrotate(u):
        return u * cos_rows[...] - pltpu.roll(u, half, 1) * sin_rows[...]

    for h in range(QW // HEAD):
        here = slice(h * HEAD, (h + 1) * HEAD)
        there = slice(G0 + h * HEAD, G0 + (h + 1) * HEAD)
        query = rows[:, here]
        grads = rows[:, there]
        scores = dot(query, keys, NTD) * SCALE + bias[...]
        weight = jnp.exp(scores - jnp.max(scores, axis=1, keepdims=True))
        prob = weight * (1.0 / jnp.sum(weight, axis=1, keepdims=True))
        rounded = prob.astype(BF)
        attended = dot(rounded, values).astype(BF)
        back[:, there] = attended
        delta = jnp.sum(grads.astype(F32) * attended.astype(F32), axis=1, keepdims=True)
        prob_grad = dot(grads, values, NTD)
        score_grad = (prob * (prob_grad - delta)).astype(BF)
        back[:, here] = unrotate(dot(score_grad, keys) * SCALE).astype(BF)
        key_grad = key_grad + dot(score_grad, query, TN)
        value_grad = value_grad + dot(rounded, grads, TN)
    back[:, K0:V0] = unrotate(key_grad * SCALE).astype(BF)
    back[:, V0:G0] = value_grad.astype(BF)
    for k in range(TARGETS):
        out_ref[live[k]] = back[k * PAIR : (k + 1) * PAIR, :]


def attend(live, offsets, got, cos_table, sin_table, doc_col, doc_row, pos_col, pos_row, *tokens):
    return pl.pallas_call(
        attend_kernel,
        in_specs=[smem_spec(), smem_spec(), any_spec()] + [vmem_spec()] * 6 + [any_spec()] * 3,
        out_specs=vmem_spec(),
        out_shape=jax.ShapeDtypeStruct((N_CTX, PAIR, COLS), BF),
        scratch_shapes=[
            pltpu.VMEM((TOK, COLS), BF),
            pltpu.VMEM((TOK, COLS), BF),
            pltpu.VMEM((TOK, TOK), F32),
            pltpu.VMEM((TOK, HEAD), F32),
            pltpu.VMEM((TOK, HEAD), F32),
            pltpu.SemaphoreType.DMA((TARGETS,)),
        ],
        compiler_params=params(28),
        cost_estimate=cost(4e9, 6e6),
        name="attend",
    )(live, offsets, got, cos_table, sin_table, doc_col, doc_row, pos_col, pos_row, *tokens)


def stage_kernel(where, after, wq_ref, wk_ref, wv_ref, out_ref, token):
    token[...] = jnp.zeros_like(token)
    out_ref[:, :K0] = wq_ref[...]
    out_ref[:, K0:V0] = wk_ref[...]
    out_ref[:, V0:] = wv_ref[...]


def stage_weights(where, after, at, count, wq, wk, wv):
    span = WIDTH // NT
    block = lambda i, where: (related(where[3], at + i), 0)
    return pl.pallas_call(
        stage_kernel,
        grid_spec=pltpu.PrefetchScalarGridSpec(
            num_scalar_prefetch=1,
            grid=(count,),
            in_specs=[
                any_spec(),
                pl.BlockSpec((span, QW), block),
                pl.BlockSpec((span, KW), block),
                pl.BlockSpec((span, KW), block),
            ],
            out_specs=[pl.BlockSpec((span, G0), lambda i, *_: (i, 0)), TOKEN_SPEC],
        ),
        out_shape=[jax.ShapeDtypeStruct((count * span, G0), BF), TOKEN],
        compiler_params=params(12),
        cost_estimate=cost(1, 3e6 * count),
        name="stage_weights",
    )(where, after, wq, wk, wv)


def restore_kernel(targets, got_ref, rows_ref, out_ref, packed, sems):
    copies = fetch_blocks(got_ref, targets, packed, sems)
    slot = lax.broadcasted_iota(I32, (TOK, TOK), 1)
    one_hot = jnp.where(slot == rows_ref[...], 1.0, 0.0).astype(BF)
    cut = TOK // 2
    for copy in copies[: TARGETS // 2]:
        copy.wait()
    total = dot(one_hot[:, :cut], packed[:cut, :])
    for copy in copies[TARGETS // 2 :]:
        copy.wait()
    out_ref[...] = (total + dot(one_hot[:, cut:], packed[cut:, :])).astype(BF)


def restore(targets, got, rows):
    return pl.pallas_call(
        restore_kernel,
        in_specs=[smem_spec(), any_spec(), vmem_spec()],
        out_specs=vmem_spec(),
        out_shape=jax.ShapeDtypeStruct((TOK, COLS), BF),
        scratch_shapes=[pltpu.VMEM((TOK, COLS), BF), pltpu.SemaphoreType.DMA((TARGETS,))],
        compiler_params=params(16),
        cost_estimate=cost(0.7e9, 4e6),
        name="restore",
    )(targets, got, rows)


def input_grad_kernel(after, dy_ref, w_ref, *outs):
    total = dot(dy_ref[:, :G0], w_ref[...], NTD).astype(BF)
    if len(outs) == 1:
        outs[0][...] = total
    else:
        outs[0][...] = total[: TOK // 2]
        outs[1][...] = total[TOK // 2 :]


def input_grad(after, at, count, dy, weights, split=False):
    span = WIDTH // NT
    if split:
        out_shape = [jax.ShapeDtypeStruct((TOK // 2, span), BF)] * 2
        out_specs = [pl.BlockSpec((TOK // 2, span), lambda i: (0, 0))] * 2
    else:
        out_shape = jax.ShapeDtypeStruct((count * TOK, span), BF)
        out_specs = pl.BlockSpec((TOK, span), lambda i: (i, 0))
    return pl.pallas_call(
        input_grad_kernel,
        grid=(count,),
        in_specs=[
            any_spec(),
            pl.BlockSpec((TOK, COLS), lambda i: (0, 0)),
            pl.BlockSpec((span, G0), lambda i: (at + 2 * i, 0)),
        ],
        out_specs=out_specs,
        out_shape=out_shape,
        compiler_params=params(20),
        cost_estimate=cost(0.8e9 * count, 5e6 * count),
        name="input_grad",
    )(after, dy, weights)


def weight_grad_kernel(after, own, peer, xa0, xa1, c0, c1, b00, b01, b02, b03, b10, b11, b12, b13, *outs):
    wide = lambda ref: jnp.concatenate([ref[j] for j in range(NZ)], axis=1)
    join = lambda refs: jnp.concatenate([ref[0] for ref in refs], axis=1)
    first = dot(own[:, V0:G0], wide(xa0), TN) + dot(peer[:, V0:G0], wide(xa1), TN)
    second = dot(own[:, G0:], wide(c0), TN) + dot(peer[:, G0:], wide(c1), TN)
    third = dot(own[:, :V0], join([b00, b01, b02, b03]), TN) + dot(
        peer[:, :V0], join([b10, b11, b12, b13]), TN
    )
    if len(outs) == 4:
        a0, a1, b0, b1 = outs
        a0[:KW, :] = first.astype(BF)
        a0[KW:, :] = second[: CUT - KW].astype(BF)
        a1[...] = second[CUT - KW :].astype(BF)
        b0[...] = third[:CUT].astype(BF)
        b1[...] = third[CUT:].astype(BF)
    else:
        a, b = outs
        a[:KW, :] = first.astype(BF)
        a[KW:, :] = second.astype(BF)
        b[...] = third.astype(BF)


def weight_grad(after, at, count, split, own, peer, xk, xr, ck, cr):
    wide = NZ * HEAD
    whole = lambda i: (0, 0)
    spec_a = pl.BlockSpec((NZ, TOK, HEAD), lambda i: (at + 2 * i, 0, 0))
    specs_b = [
        pl.BlockSpec((1, TOK, HEAD), functools.partial(lambda j, i: (j * NZ + at + 2 * i, 0, 0), j))
        for j in range(NX)
    ]
    if split:
        out_shape = [jax.ShapeDtypeStruct((CUT, wide), BF)] * 4
        out_specs = [pl.BlockSpec((CUT, wide), whole)] * 4
    else:
        out_shape = [jax.ShapeDtypeStruct((count * HALF, wide), BF)] * 2
        out_specs = [pl.BlockSpec((HALF, wide), lambda i: (i, 0))] * 2
    return pl.pallas_call(
        weight_grad_kernel,
        grid=(count,),
        in_specs=[any_spec(), pl.BlockSpec((TOK, COLS), whole), pl.BlockSpec((TOK, COLS), whole)]
        + [spec_a] * 4
        + specs_b
        + specs_b,
        out_specs=out_specs,
        out_shape=out_shape,
        compiler_params=params(28),
        cost_estimate=cost(1.4e9 * count, 6e6 * count),
        name="weight_grad",
    )(after, own, peer, xk, xr, ck, cr, xk, xk, xk, xk, xr, xr, xr, xr)


def near_kernel(count, *refs):
    for g in range(count):
        near, below, above = refs[3 * g : 3 * g + 3]
        up, down = refs[3 * count + 2 * g : 3 * count + 2 * g + 2]
        rows = up.shape[0]
        cut = rows // 2
        up[:cut] = (near[:cut].astype(F32) + below[...].astype(F32)).astype(BF)
        up[cut:] = near[cut:rows]
        down[:cut] = near[rows : rows + cut]
        down[cut:] = (near[rows + cut :].astype(F32) + above[...].astype(F32)).astype(BF)


def add_near(*groups):
    flat = [value for group in groups for value in group]
    shapes = []
    for near, _, _ in groups:
        shapes += [jax.ShapeDtypeStruct((near.shape[0] // 2, near.shape[1]), BF)] * 2
    return pl.pallas_call(
        functools.partial(near_kernel, len(groups)),
        in_specs=[vmem_spec()] * len(flat),
        out_specs=[vmem_spec()] * len(shapes),
        out_shape=shapes,
        compiler_params=params(16),
        cost_estimate=cost(1e6, 5e6),
        name="add_near",
    )(*flat)


def total_kernel(own_a, up_a, down_a, own_b, up_b, down_b, *outs):
    for g, (own, up, down) in enumerate(((own_a, up_a, down_a), (own_b, up_b, down_b))):
        total = own[...].astype(F32) + up[...].astype(F32) + down[...].astype(F32)
        for place in range(NZ):
            ref = outs[4 * g + place]
            ref[...] = total[:, place * HEAD : (place + 1) * HEAD].astype(ref.dtype)


def add_total(own_a, near_a, own_b, near_b):
    one = [jax.ShapeDtypeStruct((HALF, HEAD), F32 if place == OWN else BF) for place in range(NZ)]
    return pl.pallas_call(
        total_kernel,
        in_specs=[vmem_spec()] * 6,
        out_specs=[vmem_spec()] * 8,
        out_shape=one + one,
        compiler_params=params(16),
        cost_estimate=cost(1e6, 5e6),
        name="add_total",
    )(own_a, *near_a, own_b, *near_b)


def finish_kernel(*refs):
    ins, (rows, query, key, value, out) = refs[:11], refs[11:]
    rows[...] = sum(ref[...].astype(F32) for ref in ins[8:]).astype(BF)
    a, b = (sum(ref[...].astype(F32) for ref in ins[4 * g : 4 * g + 4]).T for g in range(2))
    value[...] = a[:, :KW].astype(BF)
    out[...] = a[:, KW:].astype(BF)
    query[...] = b[:, :QW].astype(BF)
    key[...] = b[:, QW:].astype(BF)


def finish(own_a, got_a, own_b, got_b, own_y, got_y):
    shape = lambda n: jax.ShapeDtypeStruct((HEAD, n), BF)
    return pl.pallas_call(
        finish_kernel,
        in_specs=[vmem_spec()] * 11,
        out_specs=[vmem_spec()] * 5,
        out_shape=[jax.ShapeDtypeStruct(own_y.shape, BF), shape(QW), shape(KW), shape(KW), shape(QW)],
        compiler_params=params(16),
        cost_estimate=cost(1e6, 6e6),
        name="finish",
    )(own_a, *got_a, own_b, *got_b, own_y, *got_y)


def shift(value, axis, by):
    n = lax.axis_size(axis)
    return lax.ppermute(value, axis, [(i, (i + by) % n) for i in range(n)])


def both_ways(up, down, axis):
    return shift(up, axis, 1), shift(down, axis, -1)


def all_ways(a, a_axis, b, b_axis):
    far = shift(a[FAR], a_axis, 2), shift(b[FAR], b_axis, 2)
    up = shift(a[UP], a_axis, 1), shift(b[UP], b_axis, 1)
    down = shift(a[DOWN], a_axis, -1), shift(b[DOWN], b_axis, -1)
    return tuple(zip(far, up, down))


def on_device(x, wq, wk, wv, wo, c, piece_doc, piece_offset, doc_owner):
    ix, iz, ic, iy = (lax.axis_index(a) for a in ("x", "z", "c", "tp"))
    me = (ix * NZ + iz) * NC + ic
    cos_table, sin_table = rotary_tables()
    sent, token_p = project(
        me.reshape(1), piece_doc, piece_offset, doc_owner, x, c, wq, wk, wv, wo, cos_table, sin_table
    )
    got = lax.all_to_all(sent, CTX, split_axis=0, concat_axis=0, tiled=True)
    where = jnp.stack([ix, iz, ic, iy]).astype(I32)
    xk, xs, ck, cs, token_x = regroup(where, token_p, x, c)
    w_far, token_f = stage_weights(where, token_p, FAR, 1, wq, wk, wv)
    w_rest, token_r = stage_weights(where, token_p, UP, 3, wq, wk, wv)
    xr = shift(xs, "c", 1)
    cr = shift(cs, "c", 1)

    doc_grid = piece_doc.reshape(N_CTX, PIECES)
    own_doc = lax.dynamic_slice_in_dim(piece_doc, me * PIECES, PIECES)
    doc_ids = jnp.arange(doc_owner.shape[0], dtype=I32)
    own_owner = jnp.sum(jnp.where(own_doc[:, None] == doc_ids[None, :], doc_owner[None, :], 0), axis=1)
    ids = jnp.arange(PIECES, dtype=I32)
    order_key = own_owner * PIECES + ids
    slot = jnp.sum((order_key[None, :] < order_key[:, None]).astype(I32), axis=1)
    blocks = jnp.arange(TARGETS, dtype=I32) * (PAIR // PIECE)
    targets = jnp.sum(jnp.where(blocks[:, None] == slot[None, :], own_owner[None, :], 0), axis=1)
    within = jnp.arange(PIECE, dtype=I32)
    packed_row = (slot[:, None] * PIECE + within[None, :]).reshape(TOK, 1)

    mine_doc = doc_owner == me
    doc_rank = jnp.sum((mine_doc[None, :] & (doc_ids[None, :] < doc_ids[:, None])).astype(I32), axis=1)
    four = jnp.arange(4, dtype=I32)
    my_docs = jnp.sum(
        jnp.where(mine_doc[None, :] & (doc_rank[None, :] == four[:, None]), doc_ids[None, :], 0), axis=1
    )
    mine = jnp.any(doc_grid[None, :, :] == my_docs[:, None, None], axis=0)
    before = (ids[:, None] < ids[None, :]).astype(BF)
    rank_in = jnp.dot(mine.astype(BF), before, preferred_element_type=F32).astype(I32)
    is_live = jnp.any(mine, axis=1)
    sources = jnp.arange(N_CTX, dtype=I32)
    live_rank = jnp.sum((is_live[None, :] & (sources[None, :] < sources[:, None])).astype(I32), axis=1)
    kth = jnp.arange(TARGETS, dtype=I32)
    live = jnp.sum(
        jnp.where(is_live[None, :] & (live_rank[None, :] == kth[:, None]), sources[None, :], 0), axis=1
    )
    index = jnp.where(mine, live_rank[:, None] * (PAIR // PIECE) + rank_in, -1).reshape(1, -1)
    chosen = index == ids[:, None]
    live_doc = jnp.sum(jnp.where(chosen, piece_doc[None, :], 0), axis=1)
    live_offset = jnp.sum(jnp.where(chosen, piece_offset[None, :], 0), axis=1)
    row_doc = jnp.repeat(live_doc, PIECE)
    row_pos = (live_offset[:, None] + within[None, :]).reshape(-1)

    back = attend(
        live,
        live_offset,
        got,
        cos_table,
        sin_table,
        row_doc[:, None],
        row_doc[None, :],
        row_pos[:, None],
        row_pos[None, :],
        token_x,
        token_f,
        token_r,
    )
    home = lax.all_to_all(back, CTX, split_axis=0, concat_axis=0, tiled=True)
    dy = restore(targets, home, packed_row)
    peer = shift(dy, "c", 1)
    y0, y1 = input_grad(dy, 0, 1, dy, w_far, split=True)
    y_far = both_ways(y0, y1, "tp")
    a0, a1, b0, b1 = weight_grad(y0, FAR, 1, True, dy, peer, xk, xr, ck, cr)
    a_far = both_ways(a0, a1, "x")
    b_far = both_ways(b0, b1, "z")
    a_near, b_near = weight_grad(a0, UP, 2, False, dy, peer, xk, xr, ck, cr)
    y_near = input_grad(a_near, UP - 1, 2, dy, w_rest)
    sums = add_near((a_near, *a_far), (b_near, *b_far))
    a_got = both_ways(*sums[:2], "x")
    b_got = both_ways(*sums[2:], "z")
    y_sums = add_near((y_near, *y_far))
    y_got = both_ways(*y_sums, "tp")
    a_own, b_own = weight_grad(y_near, OWN, 1, False, dy, peer, xk, xr, ck, cr)
    y_own = input_grad(a_own, OWN - 1, 1, dy, w_rest)
    parts = add_total(a_own, a_got, b_own, b_got)
    a_got, b_got = all_ways(parts[:4], "z", parts[4:], "x")
    grad_in, grad_query, grad_key, grad_value, grad_out = finish(
        parts[OWN], a_got, parts[4 + OWN], b_got, y_own, y_got
    )
    return grad_in, grad_query, grad_key, grad_value, grad_out


def solution(mesh):
    fine = Mesh(mesh.devices.reshape(NX, NZ, NC, NT), ("x", "z", "c", "tp"))
    column = P(None, "tp")
    both = P(CTX, "tp")
    return jax.shard_map(
        on_device,
        mesh=fine,
        in_specs=(P(CTX, None), column, column, column, column, P(CTX, None), P(), P(), P()),
        out_specs=(both,) * 5,
        check_vma=False,
    )
```

```python
import functools
import math

import jax
import jax.numpy as jnp
import numpy as np
from jax import lax
from jax.experimental import pallas as pl
from jax.experimental.pallas import tpu as pltpu
from jax.sharding import Mesh, PartitionSpec as P


HEAD = 128
PIECE = 8
ROPE_BASE = 500000.0
FILL = -1e30
NX, NZ, NC, NT = 4, 4, 2, 4
CTX = ("x", "z", "c")
N_CTX = NX * NZ * NC
TOK = 512
WIDTH = 4096
QW = 512
KW = 128
COLS = 1280
K0, V0, G0 = 512, 640, 768
PAIR = 32
TARGETS = 16
PIECES = TOK // PIECE
MAX_POS = 512
HALF = 640
CUT = HALF // 2
FAR, UP, OWN, DOWN = 0, 1, 2, 3
SCALE = 1.0 / math.sqrt(HEAD)
BF = jnp.bfloat16
F32 = jnp.float32
I32 = jnp.int32
NN = (((1,), (0,)), ((), ()))
NTD = (((1,), (1,)), ((), ()))
TN = (((0,), (0,)), ((), ()))
TOKEN = jax.ShapeDtypeStruct((8, HEAD), F32)
TOKEN_SPEC = pl.BlockSpec((8, HEAD), lambda *_: (0, 0))


def dot(a, b, dims=NN):
    return lax.dot_general(a, b, dims, preferred_element_type=F32)


def vmem_spec():
    return pl.BlockSpec(memory_space=pltpu.VMEM)


def smem_spec():
    return pl.BlockSpec(memory_space=pltpu.SMEM)


def any_spec():
    return pl.BlockSpec(memory_space=pl.ANY)


def params(mib):
    return pltpu.CompilerParams(vmem_limit_bytes=mib * 1024 * 1024)


def cost(flops, nbytes):
    return pl.CostEstimate(flops=int(flops), bytes_accessed=int(nbytes), transcendentals=0)


def rotary_tables():
    half = HEAD // 2
    frequency = np.float32(ROPE_BASE) ** (-2.0 * np.arange(half, dtype=np.float32) / np.float32(HEAD))
    angles = np.arange(MAX_POS, dtype=np.float32)[:, None] * frequency.astype(np.float32)[None, :]
    cosine, sine = np.cos(angles), np.sin(angles)
    return (
        jnp.asarray(np.concatenate([cosine, cosine], axis=1).astype(np.float32)),
        jnp.asarray(np.concatenate([-sine, sine], axis=1).astype(np.float32)),
    )


def related(coordinate, order):
    return (coordinate + 2 - order) & 3


def store_blocks(rows, target, which, sems):
    copies = [
        pltpu.make_async_copy(rows.at[pl.ds(k * PAIR, PAIR)], target.at[which[k]], sems.at[k])
        for k in range(TARGETS)
    ]
    for copy in copies:
        copy.start()
    return copies


def project_kernel(
    me,
    piece_doc,
    piece_offset,
    doc_owner,
    x_hbm,
    c_hbm,
    wq_hbm,
    wk_hbm,
    wv_hbm,
    wo_hbm,
    cos_table,
    sin_table,
    out_ref,
    token,
    x_ref,
    c_ref,
    wq_ref,
    wkv_ref,
    wo_ref,
    made,
    packed,
    final,
    slot_of,
    count,
    first,
    targets,
    load_sems,
    sems,
):
    span = 2 * HEAD
    copy = pltpu.make_async_copy
    token[...] = jnp.zeros_like(token)
    get_x = copy(x_hbm, x_ref, load_sems.at[0])
    get_k = copy(wk_hbm, wkv_ref.at[:, pl.ds(0, KW)], load_sems.at[1])
    get_v = copy(wv_hbm, wkv_ref.at[:, pl.ds(KW, KW)], load_sems.at[2])
    get_c = copy(c_hbm, c_ref, load_sems.at[3])

    def part(i, source, into, sem):
        at = pl.ds(pl.multiple_of(i * span, span), span)
        return copy(source.at[:, at], into.at[i], load_sems.at[sem + i])

    get_x.start()
    get_k.start()
    get_v.start()
    for i in range(2):
        part(i, wq_hbm, wq_ref, 4).start()
    get_c.start()
    for i in range(2):
        part(i, wo_hbm, wo_ref, 6).start()

    for o in range(N_CTX):
        count[o] = 0
    for i in range(PIECES):
        owner = doc_owner[piece_doc[me[0] * PIECES + i]]
        slot_of[i] = owner * PIECES + count[owner]
        count[owner] = count[owner] + 1
    run = jnp.int32(0)
    for o in range(N_CTX):
        first[o] = run
        targets[run >> 2] = jnp.int32(o)
        run = run + count[o]
    for i in range(PIECES):
        key = slot_of[i]
        slot_of[i] = (first[key >> 6] + (key & (PIECES - 1))) * PIECE

    def pack(base, rotated):
        for i in range(PIECES):
            to = pl.multiple_of(slot_of[i], PIECE)
            here = slice(i * PIECE, (i + 1) * PIECE)
            if rotated:
                at = pl.multiple_of(piece_offset[me[0] * PIECES + i], PIECE)
                cosine = cos_table[pl.ds(at, PIECE), :]
                sine = sin_table[pl.ds(at, PIECE), :]
            for h in range(2):
                u = made[here, h * HEAD : (h + 1) * HEAD]
                if h < rotated:
                    u = u * cosine + pltpu.roll(u, HEAD // 2, 1) * sine
                packed[pl.ds(to, PIECE), h * HEAD : (h + 1) * HEAD] = u
        final[:, pl.ds(base, span)] = packed[...].astype(BF)

    get_x.wait()
    get_k.wait()
    get_v.wait()
    made[...] = dot(x_ref[...], wkv_ref[...])
    pack(K0, 1)

    @pl.loop(0, 2)
    def _(i):
        part(i, wq_hbm, wq_ref, 4).wait()
        made[...] = dot(x_ref[...], wq_ref[i])
        pack(pl.multiple_of(i * span, span), 2)

    get_c.wait()

    @pl.loop(0, 2)
    def _(i):
        part(i, wo_hbm, wo_ref, 6).wait()
        made[...] = dot(c_ref[...], wo_ref[i])
        pack(pl.multiple_of(G0 + i * span, span), 0)

    for each in store_blocks(final, out_ref, targets, sems):
        each.wait()


def project(me, piece_doc, piece_offset, doc_owner, x, c, wq, wk, wv, wo, cos_table, sin_table):
    span = 2 * HEAD
    smem = pltpu.SMEM
    return pl.pallas_call(
        project_kernel,
        in_specs=[smem_spec()] * 4 + [any_spec()] * 6 + [vmem_spec()] * 2,
        out_specs=[any_spec(), vmem_spec()],
        scratch_shapes=[
            pltpu.VMEM((TOK, WIDTH), BF),
            pltpu.VMEM((TOK, WIDTH), BF),
            pltpu.VMEM((2, WIDTH, span), BF),
            pltpu.VMEM((WIDTH, 2 * KW), BF),
            pltpu.VMEM((2, WIDTH, span), BF),
            pltpu.VMEM((TOK, span), F32),
            pltpu.VMEM((TOK, span), F32),
            pltpu.VMEM((TOK, COLS), BF),
            smem((PIECES,), I32),
            smem((N_CTX,), I32),
            smem((N_CTX,), I32),
            smem((N_CTX,), I32),
            pltpu.SemaphoreType.DMA((8,)),
            pltpu.SemaphoreType.DMA((TARGETS,)),
        ],
        out_shape=[jax.ShapeDtypeStruct((N_CTX, PAIR, COLS), BF), TOKEN],
        compiler_params=params(60),
        cost_estimate=cost(6e9, 24e6),
        name="project",
    )(me, piece_doc, piece_offset, doc_owner, x, c, wq, wk, wv, wo, cos_table, sin_table)


def regroup_kernel(where, after, x_ref, c_ref, xk_ref, xs_ref, ck_ref, cs_ref, token):
    token[...] = jnp.zeros_like(token)
    core = where[2]
    for i in range(NZ):
        base = related(where[1], i) * 2
        keep = pl.ds(pl.multiple_of((base + core) * HEAD, HEAD), HEAD)
        send = pl.ds(pl.multiple_of((base + 1 - core) * HEAD, HEAD), HEAD)
        xk_ref[i] = x_ref[:, keep]
        xs_ref[i] = x_ref[:, send]
        ck_ref[i] = c_ref[:, keep]
        cs_ref[i] = c_ref[:, send]


def regroup(where, after, x, c):
    part = pl.BlockSpec((TOK, WIDTH // NX), lambda i, where: (0, related(where[0], i)))
    half = jax.ShapeDtypeStruct((NX * NZ, TOK, HEAD), BF)
    return pl.pallas_call(
        regroup_kernel,
        grid_spec=pltpu.PrefetchScalarGridSpec(
            num_scalar_prefetch=1,
            grid=(NX,),
            in_specs=[any_spec(), part, part],
            out_specs=[pl.BlockSpec((NZ, TOK, HEAD), lambda i, where: (i, 0, 0))] * 4 + [TOKEN_SPEC],
        ),
        out_shape=[half] * 4 + [TOKEN],
        compiler_params=params(16),
        cost_estimate=cost(1, 17e6),
        name="regroup",
    )(where, after, x, c)


def fetch_blocks(source, which, rows, sems):
    copies = [
        pltpu.make_async_copy(source.at[which[k]], rows.at[pl.ds(k * PAIR, PAIR)], sems.at[k])
        for k in range(TARGETS)
    ]
    for copy in copies:
        copy.start()
    return copies


def attend_kernel(
    live,
    offsets,
    got_ref,
    cos_table,
    sin_table,
    doc_col,
    doc_row,
    pos_col,
    pos_row,
    token_x,
    token_f,
    token_r,
    out_ref,
    rows,
    back,
    bias,
    cos_rows,
    sin_rows,
    sems,
):
    copies = fetch_blocks(got_ref, live, rows, sems)
    for i in range(PIECES):
        at = pl.multiple_of(offsets[i], PIECE)
        cos_rows[i * PIECE : (i + 1) * PIECE, :] = cos_table[pl.ds(at, PIECE), :]
        sin_rows[i * PIECE : (i + 1) * PIECE, :] = sin_table[pl.ds(at, PIECE), :]
    allowed = (doc_col[...] == doc_row[...]) & (pos_row[...] <= pos_col[...])
    bias[...] = jnp.where(allowed, 0.0, FILL)
    for copy in copies:
        copy.wait()
    keys = rows[:, K0:V0]
    values = rows[:, V0:G0]
    key_grad = jnp.zeros((TOK, HEAD), F32)
    value_grad = jnp.zeros((TOK, HEAD), F32)
    half = HEAD // 2

    def unrotate(u):
        return u * cos_rows[...] - pltpu.roll(u, half, 1) * sin_rows[...]

    for h in range(QW // HEAD):
        here = slice(h * HEAD, (h + 1) * HEAD)
        there = slice(G0 + h * HEAD, G0 + (h + 1) * HEAD)
        query = rows[:, here]
        grads = rows[:, there]
        scores = dot(query, keys, NTD) * SCALE + bias[...]
        weight = jnp.exp(scores - jnp.max(scores, axis=1, keepdims=True))
        prob = weight * (1.0 / jnp.sum(weight, axis=1, keepdims=True))
        rounded = prob.astype(BF)
        attended = dot(rounded, values).astype(BF)
        back[:, there] = attended
        delta = jnp.sum(grads.astype(F32) * attended.astype(F32), axis=1, keepdims=True)
        prob_grad = dot(grads, values, NTD)
        score_grad = (prob * (prob_grad - delta)).astype(BF)
        back[:, here] = unrotate(dot(score_grad, keys) * SCALE).astype(BF)
        key_grad = key_grad + dot(score_grad, query, TN)
        value_grad = value_grad + dot(rounded, grads, TN)
    back[:, K0:V0] = unrotate(key_grad * SCALE).astype(BF)
    back[:, V0:G0] = value_grad.astype(BF)
    for k in range(TARGETS):
        out_ref[live[k]] = back[k * PAIR : (k + 1) * PAIR, :]


def attend(live, offsets, got, cos_table, sin_table, doc_col, doc_row, pos_col, pos_row, *tokens):
    return pl.pallas_call(
        attend_kernel,
        in_specs=[smem_spec(), smem_spec(), any_spec()] + [vmem_spec()] * 6 + [any_spec()] * 3,
        out_specs=vmem_spec(),
        out_shape=jax.ShapeDtypeStruct((N_CTX, PAIR, COLS), BF),
        scratch_shapes=[
            pltpu.VMEM((TOK, COLS), BF),
            pltpu.VMEM((TOK, COLS), BF),
            pltpu.VMEM((TOK, TOK), F32),
            pltpu.VMEM((TOK, HEAD), F32),
            pltpu.VMEM((TOK, HEAD), F32),
            pltpu.SemaphoreType.DMA((TARGETS,)),
        ],
        compiler_params=params(28),
        cost_estimate=cost(4e9, 6e6),
        name="attend",
    )(live, offsets, got, cos_table, sin_table, doc_col, doc_row, pos_col, pos_row, *tokens)


def stage_kernel(where, after, wq_ref, wk_ref, wv_ref, out_ref, token):
    token[...] = jnp.zeros_like(token)
    out_ref[:, :K0] = wq_ref[...]
    out_ref[:, K0:V0] = wk_ref[...]
    out_ref[:, V0:] = wv_ref[...]


def stage_weights(where, after, at, count, wq, wk, wv):
    span = WIDTH // NT
    block = lambda i, where: (related(where[3], at + i), 0)
    return pl.pallas_call(
        stage_kernel,
        grid_spec=pltpu.PrefetchScalarGridSpec(
            num_scalar_prefetch=1,
            grid=(count,),
            in_specs=[
                any_spec(),
                pl.BlockSpec((span, QW), block),
                pl.BlockSpec((span, KW), block),
                pl.BlockSpec((span, KW), block),
            ],
            out_specs=[pl.BlockSpec((span, G0), lambda i, *_: (i, 0)), TOKEN_SPEC],
        ),
        out_shape=[jax.ShapeDtypeStruct((count * span, G0), BF), TOKEN],
        compiler_params=params(12),
        cost_estimate=cost(1, 3e6 * count),
        name="stage_weights",
    )(where, after, wq, wk, wv)


def collect_kernel(xk_hbm, xr_hbm, ck_hbm, cr_hbm, far_ref, token, sems):
    token[...] = jnp.zeros_like(token)
    pairs = []
    for i, source in enumerate((xk_hbm, xr_hbm, ck_hbm, cr_hbm)):
        pairs.append((source.at[pl.ds(FAR * NZ, NZ)], far_ref.at[pl.ds(i * NZ, NZ)]))
    for i, source in enumerate((xk_hbm, xr_hbm)):
        for j in range(NX):
            pairs.append((source.at[j * NZ + FAR], far_ref.at[4 * NZ + i * NX + j]))
    copies = [pltpu.make_async_copy(*pair, sems.at[n]) for n, pair in enumerate(pairs)]
    for copy in copies:
        copy.start()
    for copy in copies:
        copy.wait()


def collect(xk, xr, ck, cr):
    return pl.pallas_call(
        collect_kernel,
        in_specs=[any_spec()] * 4,
        out_specs=[vmem_spec(), vmem_spec()],
        out_shape=[jax.ShapeDtypeStruct((4 * NZ + 2 * NX, TOK, HEAD), BF), TOKEN],
        scratch_shapes=[pltpu.SemaphoreType.DMA((4 + 2 * NX,))],
        compiler_params=params(8),
        cost_estimate=cost(1, 6e6),
        name="collect",
    )(xk, xr, ck, cr)


def restore_kernel(targets, got_ref, rows_ref, token, out_ref, packed, sems):
    copies = fetch_blocks(got_ref, targets, packed, sems)
    slot = lax.broadcasted_iota(I32, (TOK, TOK), 1)
    one_hot = jnp.where(slot == rows_ref[...], 1.0, 0.0).astype(BF)
    cut = TOK // 2
    for copy in copies[: TARGETS // 2]:
        copy.wait()
    total = dot(one_hot[:, :cut], packed[:cut, :])
    for copy in copies[TARGETS // 2 :]:
        copy.wait()
    out_ref[...] = (total + dot(one_hot[:, cut:], packed[cut:, :])).astype(BF)


def restore(targets, got, rows, token):
    return pl.pallas_call(
        restore_kernel,
        in_specs=[smem_spec(), any_spec(), vmem_spec(), any_spec()],
        out_specs=vmem_spec(),
        out_shape=jax.ShapeDtypeStruct((TOK, COLS), BF),
        scratch_shapes=[pltpu.VMEM((TOK, COLS), BF), pltpu.SemaphoreType.DMA((TARGETS,))],
        compiler_params=params(16),
        cost_estimate=cost(0.7e9, 4e6),
        name="restore",
    )(targets, got, rows, token)


def weight_far_kernel(after, own, peer, far, a0, a1, b0, b1):
    wide = lambda i: jnp.concatenate([far[4 * i + j] for j in range(NZ)], axis=1)
    first = dot(own[:, V0:G0], wide(0), TN) + dot(peer[:, V0:G0], wide(1), TN)
    a0[:KW, :] = first.astype(BF)
    second = dot(own[:, G0:], wide(2), TN) + dot(peer[:, G0:], wide(3), TN)
    a0[KW:, :] = second[: CUT - KW].astype(BF)
    a1[...] = second[CUT - KW :].astype(BF)
    third = dot(own[:, :V0], wide(4), TN) + dot(peer[:, :V0], wide(5), TN)
    b0[...] = third[:CUT].astype(BF)
    b1[...] = third[CUT:].astype(BF)


def weight_far(after, own, peer, far):
    shape = jax.ShapeDtypeStruct((CUT, NZ * HEAD), BF)
    return pl.pallas_call(
        weight_far_kernel,
        in_specs=[any_spec()] + [vmem_spec()] * 3,
        out_specs=[vmem_spec()] * 4,
        out_shape=[shape] * 4,
        compiler_params=params(20),
        cost_estimate=cost(1.4e9, 6e6),
        name="weight_far",
    )(after, own, peer, far)


def input_grad_kernel(after, dy_ref, w_ref, *outs):
    total = dot(dy_ref[:, :G0], w_ref[...], NTD).astype(BF)
    if len(outs) == 1:
        outs[0][...] = total
    else:
        outs[0][...] = total[: TOK // 2]
        outs[1][...] = total[TOK // 2 :]


def input_grad(after, at, count, dy, weights, split=False):
    span = WIDTH // NT
    if split:
        out_shape = [jax.ShapeDtypeStruct((TOK // 2, span), BF)] * 2
        out_specs = [pl.BlockSpec((TOK // 2, span), lambda i: (0, 0))] * 2
    else:
        out_shape = jax.ShapeDtypeStruct((count * TOK, span), BF)
        out_specs = pl.BlockSpec((TOK, span), lambda i: (i, 0))
    return pl.pallas_call(
        input_grad_kernel,
        grid=(count,),
        in_specs=[
            any_spec(),
            pl.BlockSpec((TOK, COLS), lambda i: (0, 0)),
            pl.BlockSpec((span, G0), lambda i: (at + 2 * i, 0)),
        ],
        out_specs=out_specs,
        out_shape=out_shape,
        compiler_params=params(20),
        cost_estimate=cost(0.8e9 * count, 5e6 * count),
        name="input_grad",
    )(after, dy, weights)


def weight_grad_kernel(after, own, peer, xa0, xa1, c0, c1, b00, b01, b02, b03, b10, b11, b12, b13, *outs):
    wide = lambda ref: jnp.concatenate([ref[j] for j in range(NZ)], axis=1)
    join = lambda refs: jnp.concatenate([ref[0] for ref in refs], axis=1)
    first = dot(own[:, V0:G0], wide(xa0), TN) + dot(peer[:, V0:G0], wide(xa1), TN)
    second = dot(own[:, G0:], wide(c0), TN) + dot(peer[:, G0:], wide(c1), TN)
    third = dot(own[:, :V0], join([b00, b01, b02, b03]), TN) + dot(
        peer[:, :V0], join([b10, b11, b12, b13]), TN
    )
    a, b = outs
    a[:KW, :] = first.astype(BF)
    a[KW:, :] = second.astype(BF)
    b[...] = third.astype(BF)


def weight_grad(after, at, count, own, peer, xk, xr, ck, cr):
    wide = NZ * HEAD
    whole = lambda i: (0, 0)
    spec_a = pl.BlockSpec((NZ, TOK, HEAD), lambda i: (at + 2 * i, 0, 0))
    specs_b = [
        pl.BlockSpec((1, TOK, HEAD), functools.partial(lambda j, i: (j * NZ + at + 2 * i, 0, 0), j))
        for j in range(NX)
    ]
    out_shape = [jax.ShapeDtypeStruct((count * HALF, wide), BF)] * 2
    out_specs = [pl.BlockSpec((HALF, wide), lambda i: (i, 0))] * 2
    return pl.pallas_call(
        weight_grad_kernel,
        grid=(count,),
        in_specs=[any_spec(), pl.BlockSpec((TOK, COLS), whole), pl.BlockSpec((TOK, COLS), whole)]
        + [spec_a] * 4
        + specs_b
        + specs_b,
        out_specs=out_specs,
        out_shape=out_shape,
        compiler_params=params(28),
        cost_estimate=cost(1.4e9 * count, 6e6 * count),
        name="weight_grad",
    )(after, own, peer, xk, xr, ck, cr, xk, xk, xk, xk, xr, xr, xr, xr)


def near_kernel(count, *refs):
    for g in range(count):
        near, below, above = refs[3 * g : 3 * g + 3]
        up, down = refs[3 * count + 2 * g : 3 * count + 2 * g + 2]
        rows = up.shape[0]
        cut = rows // 2
        up[:cut] = (near[:cut].astype(F32) + below[...].astype(F32)).astype(BF)
        up[cut:] = near[cut:rows]
        down[:cut] = near[rows : rows + cut]
        down[cut:] = (near[rows + cut :].astype(F32) + above[...].astype(F32)).astype(BF)


def add_near(*groups):
    flat = [value for group in groups for value in group]
    shapes = []
    for near, _, _ in groups:
        shapes += [jax.ShapeDtypeStruct((near.shape[0] // 2, near.shape[1]), BF)] * 2
    return pl.pallas_call(
        functools.partial(near_kernel, len(groups)),
        in_specs=[vmem_spec()] * len(flat),
        out_specs=[vmem_spec()] * len(shapes),
        out_shape=shapes,
        compiler_params=params(16),
        cost_estimate=cost(1e6, 5e6),
        name="add_near",
    )(*flat)


def total_kernel(own_a, up_a, down_a, own_b, up_b, down_b, *outs):
    for g, (own, up, down) in enumerate(((own_a, up_a, down_a), (own_b, up_b, down_b))):
        total = own[...].astype(F32) + up[...].astype(F32) + down[...].astype(F32)
        for place in range(NZ):
            ref = outs[4 * g + place]
            ref[...] = total[:, place * HEAD : (place + 1) * HEAD].astype(ref.dtype)


def add_total(own_a, near_a, own_b, near_b):
    one = [jax.ShapeDtypeStruct((HALF, HEAD), F32 if place == OWN else BF) for place in range(NZ)]
    return pl.pallas_call(
        total_kernel,
        in_specs=[vmem_spec()] * 6,
        out_specs=[vmem_spec()] * 8,
        out_shape=one + one,
        compiler_params=params(16),
        cost_estimate=cost(1e6, 5e6),
        name="add_total",
    )(own_a, *near_a, own_b, *near_b)


def finish_kernel(*refs):
    ins, (rows, query, key, value, out) = refs[:11], refs[11:]
    rows[...] = sum(ref[...].astype(F32) for ref in ins[8:]).astype(BF)
    a, b = (sum(ref[...].astype(F32) for ref in ins[4 * g : 4 * g + 4]).T for g in range(2))
    value[...] = a[:, :KW].astype(BF)
    out[...] = a[:, KW:].astype(BF)
    query[...] = b[:, :QW].astype(BF)
    key[...] = b[:, QW:].astype(BF)


def finish(own_a, got_a, own_b, got_b, own_y, got_y):
    shape = lambda n: jax.ShapeDtypeStruct((HEAD, n), BF)
    return pl.pallas_call(
        finish_kernel,
        in_specs=[vmem_spec()] * 11,
        out_specs=[vmem_spec()] * 5,
        out_shape=[jax.ShapeDtypeStruct(own_y.shape, BF), shape(QW), shape(KW), shape(KW), shape(QW)],
        compiler_params=params(16),
        cost_estimate=cost(1e6, 6e6),
        name="finish",
    )(own_a, *got_a, own_b, *got_b, own_y, *got_y)


def shift(value, axis, by):
    n = lax.axis_size(axis)
    return lax.ppermute(value, axis, [(i, (i + by) % n) for i in range(n)])


def both_ways(up, down, axis):
    return shift(up, axis, 1), shift(down, axis, -1)


def all_ways(a, a_axis, b, b_axis):
    far = shift(a[FAR], a_axis, 2), shift(b[FAR], b_axis, 2)
    up = shift(a[UP], a_axis, 1), shift(b[UP], b_axis, 1)
    down = shift(a[DOWN], a_axis, -1), shift(b[DOWN], b_axis, -1)
    return tuple(zip(far, up, down))


def on_device(x, wq, wk, wv, wo, c, piece_doc, piece_offset, doc_owner):
    ix, iz, ic, iy = (lax.axis_index(a) for a in ("x", "z", "c", "tp"))
    me = (ix * NZ + iz) * NC + ic
    cos_table, sin_table = rotary_tables()
    sent, token_p = project(
        me.reshape(1), piece_doc, piece_offset, doc_owner, x, c, wq, wk, wv, wo, cos_table, sin_table
    )
    got = lax.all_to_all(sent, CTX, split_axis=0, concat_axis=0, tiled=True)
    where = jnp.stack([ix, iz, ic, iy]).astype(I32)
    xk, xs, ck, cs, token_x = regroup(where, token_p, x, c)
    w_far, token_f = stage_weights(where, token_p, FAR, 1, wq, wk, wv)
    w_rest, token_r = stage_weights(where, token_p, UP, 3, wq, wk, wv)
    xr = shift(xs, "c", 1)
    cr = shift(cs, "c", 1)

    doc_grid = piece_doc.reshape(N_CTX, PIECES)
    own_doc = lax.dynamic_slice_in_dim(piece_doc, me * PIECES, PIECES)
    doc_ids = jnp.arange(doc_owner.shape[0], dtype=I32)
    own_owner = jnp.sum(jnp.where(own_doc[:, None] == doc_ids[None, :], doc_owner[None, :], 0), axis=1)
    ids = jnp.arange(PIECES, dtype=I32)
    order_key = own_owner * PIECES + ids
    slot = jnp.sum((order_key[None, :] < order_key[:, None]).astype(I32), axis=1)
    blocks = jnp.arange(TARGETS, dtype=I32) * (PAIR // PIECE)
    targets = jnp.sum(jnp.where(blocks[:, None] == slot[None, :], own_owner[None, :], 0), axis=1)
    within = jnp.arange(PIECE, dtype=I32)
    packed_row = (slot[:, None] * PIECE + within[None, :]).reshape(TOK, 1)

    mine_doc = doc_owner == me
    doc_rank = jnp.sum((mine_doc[None, :] & (doc_ids[None, :] < doc_ids[:, None])).astype(I32), axis=1)
    four = jnp.arange(4, dtype=I32)
    my_docs = jnp.sum(
        jnp.where(mine_doc[None, :] & (doc_rank[None, :] == four[:, None]), doc_ids[None, :], 0), axis=1
    )
    mine = jnp.any(doc_grid[None, :, :] == my_docs[:, None, None], axis=0)
    before = (ids[:, None] < ids[None, :]).astype(BF)
    rank_in = jnp.dot(mine.astype(BF), before, preferred_element_type=F32).astype(I32)
    is_live = jnp.any(mine, axis=1)
    sources = jnp.arange(N_CTX, dtype=I32)
    live_rank = jnp.sum((is_live[None, :] & (sources[None, :] < sources[:, None])).astype(I32), axis=1)
    kth = jnp.arange(TARGETS, dtype=I32)
    live = jnp.sum(
        jnp.where(is_live[None, :] & (live_rank[None, :] == kth[:, None]), sources[None, :], 0), axis=1
    )
    index = jnp.where(mine, live_rank[:, None] * (PAIR // PIECE) + rank_in, -1).reshape(1, -1)
    chosen = index == ids[:, None]
    live_doc = jnp.sum(jnp.where(chosen, piece_doc[None, :], 0), axis=1)
    live_offset = jnp.sum(jnp.where(chosen, piece_offset[None, :], 0), axis=1)
    row_doc = jnp.repeat(live_doc, PIECE)
    row_pos = (live_offset[:, None] + within[None, :]).reshape(-1)

    back = attend(
        live,
        live_offset,
        got,
        cos_table,
        sin_table,
        row_doc[:, None],
        row_doc[None, :],
        row_pos[:, None],
        row_pos[None, :],
        token_x,
        token_f,
        token_r,
    )
    home = lax.all_to_all(back, CTX, split_axis=0, concat_axis=0, tiled=True)
    far, token_c = collect(xk, xr, ck, cr)
    dy = restore(targets, home, packed_row, token_c)
    peer = shift(dy, "c", 1)
    y0, y1 = input_grad(dy, 0, 1, dy, w_far, split=True)
    y_far = both_ways(y0, y1, "tp")
    a0, a1, b0, b1 = weight_far(y0, dy, peer, far)
    a_far = both_ways(a0, a1, "x")
    b_far = both_ways(b0, b1, "z")
    a_near, b_near = weight_grad(a0, UP, 2, dy, peer, xk, xr, ck, cr)
    y_near = input_grad(a_near, UP - 1, 2, dy, w_rest)
    sums = add_near((a_near, *a_far), (b_near, *b_far))
    a_got = both_ways(*sums[:2], "x")
    b_got = both_ways(*sums[2:], "z")
    y_sums = add_near((y_near, *y_far))
    y_got = both_ways(*y_sums, "tp")
    a_own, b_own = weight_grad(y_near, OWN, 1, dy, peer, xk, xr, ck, cr)
    y_own = input_grad(a_own, OWN - 1, 1, dy, w_rest)
    parts = add_total(a_own, a_got, b_own, b_got)
    a_got, b_got = all_ways(parts[:4], "z", parts[4:], "x")
    grad_in, grad_query, grad_key, grad_value, grad_out = finish(
        parts[OWN], a_got, parts[4 + OWN], b_got, y_own, y_got
    )
    return grad_in, grad_query, grad_key, grad_value, grad_out


def solution(mesh):
    fine = Mesh(mesh.devices.reshape(NX, NZ, NC, NT), ("x", "z", "c", "tp"))
    column = P(None, "tp")
    both = P(CTX, "tp")
    return jax.shard_map(
        on_device,
        mesh=fine,
        in_specs=(P(CTX, None), column, column, column, column, P(CTX, None), P(), P(), P()),
        out_specs=(both,) * 5,
        check_vma=False,
    )
```
